512 devices in a mesh: ax: 64 (over z, y_hi, x), rad: 8 (over y_lo, core).
Axes of the slice: x: 4, y: 8 (y_hi: 2, y_lo: 4; y = y_hi * 4 + y_lo), z: 8, core: 2. Of those that a mesh axis runs over, the one named last changes fastest.
Arguments:
- parcel_motion: float32 [6, 1048576], P(None, ('ax', 'rad')), may hold values from -6 to 6
- parcel_size: float32 [1048576], P(('ax', 'rad')), may hold values from 0.5 to 2
- parcel_block: int32 [16384], P(('ax', 'rad')), may hold values from 0 to 511, as said below
- parcel_offset: int32 [1048576], P(('ax', 'rad')), may hold values from 0 to 127
- gas_velocity: float32 [3, 1024, 4096], P(None, 'ax', 'rad'), may hold values from -6 to 6
- pressure: float32 [1024, 4096], P('ax', 'rad'), may hold values from -6 to 6
- block_cols: int32 [64, 512, 4], P('ax', 'rad'), may hold values from 0 to 511
- block_kinds: int32 [64, 512, 4], P('ax', 'rad'), may hold values from 0 to 7
- block_table: float32 [8, 128, 128], replicated, may hold values from -0.5 to 0.5
- send_axial: int32 [64, 8, 2, 64], P('ax', 'rad'), may hold values from 0 to 2047, as said below
- send_radial: int32 [64, 8, 2, 32], P('ax', 'rad'), may hold values from 0 to 2047, as said below
- send_counts: int32 [64, 8, 4], P('ax', 'rad'), may hold values from 0 to 64, as said below
Outputs:
- motion_out: float32 [6, 1048576], P(None, ('ax', 'rad'))
- arrivals_axial: float32 [64, 8, 2, 7, 64], P('ax', 'rad')
- arrivals_radial: float32 [64, 8, 2, 7, 32], P('ax', 'rad')
- gas_out: float32 [3, 1024, 4096], P(None, 'ax', 'rad')
- liquid_load: float32 [1024, 4096], P('ax', 'rad')
- pressure_image: float32 [1024, 4096], P('ax', 'rad')
The draws below stay inside these ranges and needn't reach their ends.
Inputs may be any that keep to these rules, and one draw needn't show every extreme that they name: `parcel_block`: most of a device's parcel blocks lie in cell blocks of its own radial group; the others lie in other radial groups of the slab. `send_axial`: each device's lists (both axial and both radial together) hold distinct indices of that device's parcels; entries past the counts are unused. `send_radial`: disjoint from the device's axial lists, see send_axial. `send_counts`: axial counts are at most 64, radial ones at most 32; devices of radial group 0 send full lists in all four directions.
All inputs are finite; a program needn't handle non-finite values.
Results may differ from the reference program's by a relative error of at most 0.000084.
Values sent between devices are 32-bit elements; how exact they have to be, the bound alone decides.
A program may use at most 64 MiB of HBM per device.

```python
import math
import jax
import jax.numpy as jnp
from jax import lax

BLOCK = 128
PARCEL_GROUP = 64
RC = 512
AZ = 16
NPB = 32
K = 4
NT = 8
NB = 64
P_DEV = 2048
CAP_AX = 64
CAP_RAD = 32
ZLEN = 1024
RLEN = 4096
PARCELS = 1048576
PBLOCKS = 16384
N_AX = 64
N_RAD = 8


def parcel_order(key):
    keys = jax.random.split(jax.random.fold_in(key, 11), N_AX * N_RAD)
    return jax.vmap(lambda single: jax.random.permutation(single, P_DEV))(keys).astype(jnp.int32)


def draw_parcel_block(key, part):
    index = jnp.arange(PBLOCKS, dtype=jnp.int32)
    radial = index // NPB % N_RAD
    within = index % NPB
    local = jax.random.randint(jax.random.fold_in(key, 31), (PBLOCKS,), 0, NB).astype(jnp.int32)
    local = jnp.where(within == 0, NB - 1, local)
    local = jnp.where(within == 1, 0, local)
    away = jax.random.randint(jax.random.fold_in(key, 37), (PBLOCKS,), 0, 8).astype(jnp.int32) == 0
    away = jnp.logical_or(away, within == NPB - 1)
    away = jnp.logical_and(away, within >= 2)
    step = jax.random.randint(jax.random.fold_in(key, 41), (PBLOCKS,), 1, N_RAD).astype(jnp.int32)
    group = jnp.where(away, (radial + step) % N_RAD, radial)
    return (group * NB + local).astype(jnp.int32)


def draw_send_axial(key, part):
    order = parcel_order(key)
    return order[:, :2 * CAP_AX].reshape(N_AX, N_RAD, 2, CAP_AX)


def draw_send_radial(key, part):
    order = parcel_order(key)
    return order[:, 2 * CAP_AX:2 * CAP_AX + 2 * CAP_RAD].reshape(N_AX, N_RAD, 2, CAP_RAD)


def draw_send_counts(key, part):
    limits = jnp.array([CAP_AX, CAP_AX, CAP_RAD, CAP_RAD], jnp.int32)
    drawn = jax.random.randint(jax.random.fold_in(key, 23), (N_AX, N_RAD, 4), 0, limits + 1)
    core = (jnp.arange(N_RAD, dtype=jnp.int32) == 0)[None, :, None]
    return jnp.where(core, limits[None, None, :], drawn).astype(jnp.int32)


def set_ends(result, key, least, largest):
    place = [jax.random.randint(jax.random.fold_in(key, axis), (), 0, length) for axis, length in enumerate(result.shape)]
    widest = result.shape.index(max(result.shape))
    neighbour = place[:widest] + [(place[widest] + 1) % result.shape[widest]] + place[widest + 1:]
    return result.at[tuple(place)].set(least).at[tuple(neighbour)].set(largest)


def shard_levels(stream_key, dims, cuts, least, high):
    def one(axis_at, parts):
        steps = jax.random.uniform(jax.random.fold_in(jax.random.fold_in(stream_key, 6), axis_at), (parts,), jnp.float32, least / len(cuts), high / len(cuts))
        return jnp.repeat(jnp.exp(steps), dims[axis_at] // parts).reshape((-1,) + (1,) * (len(dims) - axis_at - 1))

    gain = one(*cuts[0])
    for cut in cuts[1:]:
        gain = gain * one(*cut)
    return gain


def bell_draw(key, dims, scale, bound, pieces=(), kind=jnp.bfloat16):
    values = scale * jax.random.normal(key, dims, jnp.float32)
    if pieces:
        values = values * shard_levels(key, dims, pieces, -0.22, 0.18)
    return jnp.clip(values, -bound, bound).astype(kind)


def setup_inputs(seed: int = 0) -> dict:
    streams_of = jax.random.split(jax.random.key(seed), 13)
    return {
        "parcel_motion": bell_draw(streams_of[0], (6, PARCELS), 1.0, 6.0, ((1, 512),), jnp.float32),
        "parcel_size": jnp.clip(jnp.exp(math.log(2.0) - 1.3862944 * jax.random.uniform(streams_of[1], (PARCELS,), jnp.float32) ** shard_levels(streams_of[1], (PARCELS,), ((0, 512),), -0.2, 0.2)), 0.5, 2.0),
        "parcel_block": draw_parcel_block(jax.random.fold_in(streams_of[12], 71), 0),
        "parcel_offset": set_ends(jax.random.randint(streams_of[3], (PARCELS,), 0, BLOCK), jax.random.fold_in(streams_of[3], 1), 0, BLOCK - 1).astype(jnp.int32),
        "gas_velocity": bell_draw(streams_of[4], (3, ZLEN, RLEN), 1.0, 6.0, ((1, 64), (2, 8)), jnp.float32),
        "pressure": bell_draw(streams_of[5], (ZLEN, RLEN), 1.0, 6.0, ((0, 64), (1, 8)), jnp.float32),
        "block_cols": set_ends(jax.random.randint(streams_of[6], (N_AX, NB * N_RAD, K), 0, NB * N_RAD), jax.random.fold_in(streams_of[6], 1), 0, (NB * N_RAD) - 1).astype(jnp.int32),
        "block_kinds": set_ends(jax.random.randint(streams_of[7], (N_AX, NB * N_RAD, K), 0, NT), jax.random.fold_in(streams_of[7], 1), 0, NT - 1).astype(jnp.int32),
        "block_table": bell_draw(streams_of[8], (NT, BLOCK, BLOCK), BLOCK ** -0.5, 0.5, (), jnp.float32),
        "send_axial": draw_send_axial(jax.random.fold_in(streams_of[12], 71), 0),
        "send_radial": draw_send_radial(jax.random.fold_in(streams_of[12], 71), 0),
        "send_counts": draw_send_counts(jax.random.fold_in(streams_of[12], 71), 0),
    }


TOP_PRECISION = lax.Precision.HIGHEST
DRAG = 0.5
STEP = 0.5
DIAG = 6.0


def slab_blocks(field):
    lead = field.shape[:-2]
    shaped = field.reshape(lead + (N_AX, AZ, N_RAD, RC))
    shaped = jnp.moveaxis(shaped, -2, -3)
    return shaped.reshape(lead + (N_AX, N_RAD * NB, BLOCK))


def unslab(block_list):
    lead = block_list.shape[:-3]
    shaped = block_list.reshape(lead + (N_AX, N_RAD, AZ, RC))
    shaped = jnp.moveaxis(shaped, -3, -2)
    return shaped.reshape(lead + (ZLEN, RLEN))


def reference(parcel_motion, parcel_size, parcel_block, parcel_offset, gas_velocity, pressure, block_cols, block_kinds, block_table, send_axial, send_radial, send_counts):
    gas_slab = slab_blocks(gas_velocity)
    device = jnp.arange(PARCELS, dtype=jnp.int32) // P_DEV
    axial = device // N_RAD
    owner_block = jnp.repeat(parcel_block, PARCEL_GROUP)
    visited_flags = gas_slab[:, axial, owner_block, parcel_offset]
    velocity = parcel_motion[3:6]
    factor = jnp.exp(-DRAG / (parcel_size * parcel_size))
    new_vel = visited_flags + (velocity - visited_flags) * factor
    new_pos = parcel_motion[0:3] + STEP * new_vel
    motion_out = jnp.concatenate([new_pos, new_vel], axis=0)
    mass = parcel_size * parcel_size * parcel_size
    deposit = jnp.concatenate([-mass * (new_vel - velocity), mass[None]], axis=0)
    sources = jnp.zeros((4, N_AX, N_RAD * NB, BLOCK), jnp.float32)
    sources = sources.at[:, axial, owner_block, parcel_offset].add(deposit)
    sources = unslab(sources)
    gas_out = gas_velocity + sources[:3]
    liquid_load = sources[3]

    state = jnp.concatenate([motion_out, parcel_size[None]], axis=0)
    state = state.reshape(7, N_AX, N_RAD, P_DEV).transpose(1, 2, 0, 3)

    def pick(lists, counts):
        width = lists.shape[-1]
        full_state = jnp.broadcast_to(state[:, :, None, :, :], (N_AX, N_RAD, 2, 7, P_DEV))
        full_lists = jnp.broadcast_to(lists[:, :, :, None, :], (N_AX, N_RAD, 2, 7, width))
        taken = jnp.take_along_axis(full_state, full_lists, axis=4)
        live = jnp.arange(width, dtype=jnp.int32)[None, None, None, :] < counts[..., None]
        return jnp.where(live[:, :, :, None, :], taken, jnp.float32(0.0))

    out_ax = pick(send_axial, send_counts[:, :, 0:2])
    zero_ax = jnp.zeros_like(out_ax[:1, :, 0])
    from_lower = jnp.concatenate([zero_ax, out_ax[:-1, :, 0]], axis=0)
    from_upper = jnp.concatenate([out_ax[1:, :, 1], zero_ax], axis=0)
    arrivals_axial = jnp.stack([from_lower, from_upper], axis=2)

    out_rad = pick(send_radial, send_counts[:, :, 2:4])
    zero_rad = jnp.zeros_like(out_rad[:, :1, 0])
    from_inner = jnp.concatenate([zero_rad, out_rad[:, :-1, 0]], axis=1)
    from_outer = jnp.concatenate([out_rad[:, 1:, 1], zero_rad], axis=1)
    arrivals_radial = jnp.stack([from_inner, from_outer], axis=2)

    padded = jnp.pad(pressure, ((1, 1), (0, 0)))
    image = DIAG * pressure - padded[2:] - padded[:-2]
    pres_slab = slab_blocks(pressure)
    picked = pres_slab[jnp.arange(N_AX, dtype=jnp.int32)[:, None, None], block_cols]
    kinds = (block_kinds[..., None] == jnp.arange(NT, dtype=jnp.int32)).astype(jnp.float32)
    grouped = jnp.einsum('abkt,abkn->abtn', kinds, picked, precision=TOP_PRECISION)
    coupled = jnp.einsum('abtn,tmn->abm', grouped, block_table, precision=TOP_PRECISION)
    pressure_image = image + unslab(coupled)
    return motion_out, arrivals_axial, arrivals_radial, gas_out, liquid_load, pressure_image
```

```python
import functools

import jax
import jax.numpy as jnp
from jax import lax
from jax.experimental import pallas as pl
from jax.experimental.pallas import tpu as pltpu
from jax.sharding import PartitionSpec as P

MESH = pl.DeviceIdType.MESH
F32 = jnp.float32
BF16 = jnp.bfloat16
I32 = jnp.int32
HIGHEST = lax.Precision.HIGHEST
SLOTS = 16
VMEM_BYTES = 62 * 1024 * 1024
NT_DIMS = (((1,), (1,)), ((), ()))


def hdot(a, b):
    return jnp.dot(a, b, precision=HIGHEST, preferred_element_type=F32)


def split3(x):
    hi = x.astype(BF16)
    rest = x - hi.astype(F32)
    mid = rest.astype(BF16)
    lo = (rest - mid.astype(F32)).astype(BF16)
    return hi, mid, lo


def iota(shape, dim):
    return lax.broadcasted_iota(I32, shape, dim)


def lane_gather(x, index):
    return jnp.take_along_axis(x, index, axis=1)


def step_kernel(
    na,
    nr,
    pm,
    ps,
    pb,
    po,
    gas,
    pres,
    cols,
    kinds,
    table,
    sa,
    sr,
    sc,
    motion_o,
    arra_o,
    arrr_o,
    gas_o,
    liq_o,
    pim_o,
    pmv,
    psv,
    pbv,
    pov,
    gasv,
    colv,
    kindv,
    tabv,
    sav,
    srv,
    scv,
    slab,
    rows8,
    rq,
    rqs,
    rp,
    rps,
    state,
    uown,
    dp,
    sd,
    sds,
    halo,
    xs,
    xa,
    xr,
    keys,
    coup,
    p3,
    motv,
    arrav,
    arrrv,
    gasov,
    liqv,
    pimv,
    lsem,
    osem,
    rq_s,
    rq_r,
    rp_s,
    rp_r,
    pr_s,
    pr_r,
    sd_s,
    sd_r,
    ha_s,
    ha_r,
    x_s,
    x_r,
):
    a = lax.axis_index("ax")
    r = lax.axis_index("rad")
    has_prev, has_next = a > 0, a < na - 1
    has_in, has_out = r > 0, r < nr - 1

    def to(src, dst, ssem, rsem, **where):
        return pltpu.make_async_remote_copy(
            src_ref=src, dst_ref=dst, send_sem=ssem, recv_sem=rsem, device_id=where, device_id_type=MESH
        )

    barrier = pltpu.get_barrier_semaphore()
    for k in range(1, nr):
        pl.semaphore_signal(barrier, inc=1, device_id={"rad": lax.rem(r + k, nr)}, device_id_type=MESH)

    @pl.when(has_prev)
    def _():
        pl.semaphore_signal(barrier, inc=1, device_id={"ax": a - 1}, device_id_type=MESH)

    @pl.when(has_next)
    def _():
        pl.semaphore_signal(barrier, inc=1, device_id={"ax": a + 1}, device_id_type=MESH)

    loads = [
        pltpu.make_async_copy(src, dst, lsem.at[i])
        for i, (src, dst) in enumerate(
            (
                (pb, pbv),
                (po, pov),
                (gas, gasv),
                (ps, psv),
                (pm, pmv),
                (sa, sav),
                (sr, srv),
                (sc, scv),
                (pres, slab.at[r]),
                (cols, colv),
                (kinds, kindv),
                (table, tabv),
            )
        )
    ]
    for load in loads:
        load.start()

    lane8 = iota((8, 128), 1)
    sub8 = iota((8, 128), 0)
    lane16 = iota((16, 128), 1)
    low8 = lane8 < 64
    low16 = lane16 < 64

    rows8[...] = jnp.zeros((8, 128), I32)
    loads[0].wait()
    loads[1].wait()
    rows8[0:1, 0:32] = pbv[...]
    blocks = jnp.broadcast_to(rows8[0:1, :], (8, 128))
    order = jnp.bitwise_and(jnp.where(lane8 < 16, 2 * lane8, 2 * lane8 - 31), 127)
    blocks = lane_gather(blocks, order)
    owner = jnp.right_shift(blocks, 6)
    local = jnp.bitwise_and(blocks, 63)
    ident = owner * 64 + jnp.bitwise_and(local, 3) * 16 + jnp.right_shift(local, 2)
    valid = lane8 < 32
    away = jnp.where(valid & (owner != r), 1, 0)
    rank = away
    for s in (1, 2, 4, 8, 16):
        rank = rank + jnp.where(lane8 >= s, pltpu.roll(rank, s, axis=1), 0)
    rank = rank - away
    row_rank = jnp.where(away > 0, rank, -1)
    code = jnp.where(valid, (rank * 2 + away) * 1024 + ident, 0)
    col = jnp.transpose(jnp.broadcast_to(code[0:1, :], (128, 128)))[0:32, :]
    col_id = jnp.bitwise_and(col, 1023)
    col_away = jnp.bitwise_and(jnp.right_shift(col, 10), 1)
    col_rank = jnp.right_shift(col, 11)
    lane32 = iota((32, 128), 1)
    picked = jnp.where((col_away > 0) & (col_rank + SLOTS * r == lane32), col_id + 1, 0)
    ids = picked[0:8] + picked[8:16] + picked[16:24] + picked[24:32]
    for s in (4, 2, 1):
        ids = ids + pltpu.roll(ids, s, axis=0)
    to_slot = jnp.where(
        jnp.broadcast_to(row_rank[0:1, :], (SLOTS, 128)) == iota((SLOTS, 128), 0), 1.0, 0.0
    ).astype(F32)[:, 0:32]
    offsets = pov[...]
    offs_f = offsets.astype(F32)
    slot_offs = jnp.dot(
        to_slot.astype(BF16),
        jnp.concatenate([offs_f, pltpu.roll(offs_f, 64, axis=1)], axis=0).astype(BF16),
        preferred_element_type=F32,
    ).astype(I32)
    rqs[0:8, :] = jnp.where(low8, slot_offs[0:8], pltpu.roll(slot_offs[8:16], 64, axis=1))
    rqs[8:16, :] = ids

    rq[r] = jnp.zeros((16, 128), I32)
    rp[r] = jnp.zeros((3, 8, 128), F32)
    sd[r] = jnp.zeros((4, SLOTS, 128), F32)

    @pl.when(jnp.logical_not(has_prev))
    def _():
        xa[0] = jnp.zeros((8, 128), F32)
        halo[0] = jnp.zeros((8, 512), F32)

    @pl.when(jnp.logical_not(has_next))
    def _():
        xa[1] = jnp.zeros((8, 128), F32)
        halo[1] = jnp.zeros((8, 512), F32)

    @pl.when(jnp.logical_not(has_in))
    def _():
        xr[0] = jnp.zeros((8, 128), F32)

    @pl.when(jnp.logical_not(has_out))
    def _():
        xr[1] = jnp.zeros((8, 128), F32)

    pl.semaphore_wait(barrier, nr - 1 + has_prev.astype(I32) + has_next.astype(I32))

    requests = []
    for k in range(1, nr):
        c = to(rqs, rq.at[r], rq_s.at[k], rq_r.at[k], rad=lax.rem(r + k, nr))
        c.start()
        requests.append(c)

    def halo_next():
        return to(pres.at[8:16], halo.at[0], ha_s.at[0], ha_r.at[0], ax=a + 1)

    def halo_prev():
        return to(pres.at[0:8], halo.at[1], ha_s.at[1], ha_r.at[1], ax=a - 1)

    @pl.when(has_next)
    def _():
        halo_next().start()

    @pl.when(has_prev)
    def _():
        halo_prev().start()

    loads[2].wait()
    gas_rows = jnp.concatenate(
        [
            jnp.concatenate([gasv[c, :, 128 * q : 128 * q + 128] for q in range(4)], axis=0)
            for c in range(3)
        ],
        axis=1,
    )
    at_own = jnp.where(col_id == r * 64 + lane32, 1.0, 0.0).astype(F32)[:, 0:64]
    found = hdot(at_own, gas_rows)
    for c in range(3):
        part = found[:, 128 * c : 128 * c + 128]
        uown[c] = jnp.where(low16, lane_gather(part[0:16], offsets), lane_gather(part[16:32], offsets))

    for c in requests:
        c.wait_recv()
    asked = rq[0, 8:16, :]
    for s in range(1, nr):
        asked = asked + rq[s, 8:16, :]
    asked_col = jnp.transpose(jnp.broadcast_to(asked[0:1, :], (128, 128)))
    at_asked = jnp.where(asked_col == r * 64 + 1 + iota((128, 128), 1), 1.0, 0.0).astype(F32)[:, 0:64]
    found = hdot(at_asked, gas_rows)
    for s in range(nr):
        index = rq[s, 0:8, :]
        for c in range(3):
            part = found[SLOTS * s : SLOTS * s + 16, 128 * c : 128 * c + 128]
            rps[s, c] = jnp.where(low8, lane_gather(part[0:8], index), lane_gather(part[8:16], index))
    replies = []
    for k in range(1, nr):
        dst = lax.rem(r + k, nr)
        c = to(rps.at[dst], rp.at[r], rp_s.at[k], rp_r.at[k], rad=dst)
        c.start()
        replies.append(c)
    shares = []
    for k in range(1, nr):
        c = to(pres, slab.at[r], pr_s.at[k], pr_r.at[k], rad=lax.rem(r + k, nr))
        c.start()
        shares.append(c)

    loads[9].wait()
    loads[10].wait()
    cv = colv[0]
    key = kindv[0] * 512 + jnp.bitwise_and(cv, 3) * 128 + jnp.right_shift(cv, 6) * 16
    key = key + jnp.bitwise_and(jnp.right_shift(cv, 2), 15)
    rows8[4:8, 0:64] = key
    for k in range(4):
        keys[k] = jnp.transpose(jnp.broadcast_to(rows8[4 + k : 5 + k, :], (128, 128)))[0:64, :]

    loads[3].wait()
    size = psv[...]
    factor = jnp.exp(-0.5 / (size * size))
    mass = size * size * size
    loads[4].wait()
    for i in (5, 6, 7):
        loads[i].wait()
    rows8[0:2, 0:64] = sav[0, 0]
    rows8[2:4, 0:32] = srv[0, 0]
    lists = [jnp.broadcast_to(rows8[i : i + 1, :], (8, 128)) for i in range(4)]
    counts = [jnp.broadcast_to(scv[0, :, i : i + 1], (8, 128)) for i in range(4)]
    list_ax = jnp.where(low8, lists[0], pltpu.roll(lists[1], 64, axis=1))
    list_rad = jnp.where(low8, lists[2], pltpu.roll(lists[3], 64, axis=1))
    live_ax = lane8 < jnp.where(low8, counts[0], counts[1] + 64)
    live_rad = lane8 < jnp.where(low8, counts[2], counts[3] + 64)

    w_lo = jnp.where((col_away > 0) & (col_rank < 8) & (jnp.right_shift(col_id, 6) * 8 + col_rank == lane32), 1.0, 0.0)
    w_hi = jnp.where((col_away > 0) & (col_rank >= 8) & (jnp.right_shift(col_id, 6) * 8 + col_rank - 8 == lane32), 1.0, 0.0)
    w = jnp.concatenate([w_lo, w_hi], axis=0).astype(F32)[:, 0:64]

    for c in replies:
        c.wait_recv()
    answer = jnp.concatenate([rp[:, c].reshape(nr * 8, 128) for c in range(3)], axis=1)
    spread = hdot(w, answer)
    u = []
    for c in range(3):
        lo, hi = spread[0:32, 128 * c : 128 * c + 128], spread[32:64, 128 * c : 128 * c + 128]
        even = lo[0:16] + pltpu.roll(hi[0:16], 64, axis=1)
        odd = pltpu.roll(lo[16:32], 64, axis=1) + hi[16:32]
        u.append(uown[c] + jnp.where(low16, even, odd))

    cross_ax = jnp.zeros((8, 128), F32)
    cross_rad = jnp.zeros((8, 128), F32)
    tile_ax, lane_ax = jnp.right_shift(list_ax, 7), jnp.bitwise_and(list_ax, 127)
    tile_rad, lane_rad = jnp.right_shift(list_rad, 7), jnp.bitwise_and(list_rad, 127)
    is_vel = (sub8 >= 3) & (sub8 < 6)
    for t in range(16):
        row = lambda x: jnp.broadcast_to(x[t : t + 1, :], (8, 128))
        old = jnp.concatenate([pmv[:, 128 * t : 128 * t + 128], jnp.zeros((2, 128), F32)], axis=0)
        gas_t = jnp.where(sub8 == 3, row(u[0]), jnp.where(sub8 == 4, row(u[1]), row(u[2])))
        vel = gas_t + (old - gas_t) * row(factor)
        pos = old + 0.5 * pltpu.roll(vel, 5, axis=0)
        new = jnp.where(sub8 < 3, pos, jnp.where(is_vel, vel, row(size)))
        motv[:, 128 * t : 128 * t + 128] = new[0:6]
        m = row(mass)
        state[:, 128 * t : 128 * t + 128] = jnp.where(is_vel, -m * (vel - old), jnp.where(sub8 == 6, m, 0.0))
        cross_ax = jnp.where(tile_ax == t, lane_gather(new, lane_ax), cross_ax)
        cross_rad = jnp.where(tile_rad == t, lane_gather(new, lane_rad), cross_rad)
    cross_ax = jnp.where(live_ax, cross_ax, 0.0)
    cross_rad = jnp.where(live_rad, cross_rad, 0.0)
    xs[0] = cross_ax
    xs[1] = pltpu.roll(cross_ax, 64, axis=1)
    xs[2] = cross_rad
    xs[3] = pltpu.roll(cross_rad, 64, axis=1)

    def crossing(i):
        dst = (xa.at[0], xa.at[1], xr.at[0], xr.at[1])[i]
        where = ({"ax": a + 1}, {"ax": a - 1}, {"rad": r + 1}, {"rad": r - 1})[i]
        return to(xs.at[i], dst, x_s.at[i], x_r.at[i], **where)

    sends_to = (has_next, has_prev, has_out, has_in)
    comes_from = (has_prev, has_next, has_in, has_out)
    for i in range(4):

        @pl.when(sends_to[i])
        def _(i=i):
            crossing(i).start()

    out_motion = pltpu.make_async_copy(motv, motion_o, osem.at[0])
    out_motion.start()

    sub128 = iota((128, 128), 0)
    for t in range(16):
        d = state[:, 128 * t : 128 * t + 128]
        both = jnp.concatenate([jnp.where(low8, d, 0.0), jnp.where(low8, 0.0, d)], axis=0)
        cells = jnp.where(
            jnp.broadcast_to(offsets[t : t + 1, :], (128, 128)) == sub128, 1.0, 0.0
        ).astype(BF16)
        sums = lax.dot_general(
            jnp.concatenate(split3(both), axis=0), cells, NT_DIMS, preferred_element_type=F32
        )
        sums = sums[0:16] + sums[16:32] + sums[32:48]
        dp[t] = sums[0:8]
        dp[16 + t] = sums[8:16]
    by_comp = jnp.concatenate([dp[:, 3 + c, :] for c in range(4)], axis=1)
    slotted = hdot(to_slot, by_comp)
    for c in range(4):
        sds[c] = slotted[:, 128 * c : 128 * c + 128]
    deposits = []
    for k in range(1, nr):
        c = to(sds, sd.at[r], sd_s.at[k], sd_r.at[k], rad=lax.rem(r + k, nr))
        c.start()
        deposits.append(c)

    loads[8].wait()
    loads[11].wait()
    for c in shares:
        c.wait_recv()
    slab_rows = jnp.concatenate(
        [slab[:, :, 128 * q : 128 * q + 128].reshape(nr * 16, 128) for q in range(4)], axis=0
    )
    p3[...] = jnp.concatenate(split3(slab_rows), axis=1)
    coup[...] = jnp.zeros((64, 128), F32)
    lane64 = iota((64, 128), 1)

    def kind_step(t, carry):
        chosen = []
        for q in range(4):
            want = t * 512 + q * 128 + lane64
            g = jnp.where(keys[0] == want, 1.0, 0.0)
            for k in range(1, 4):
                g = g + jnp.where(keys[k] == want, 1.0, 0.0)
            chosen.append(g.astype(BF16))
        three = jnp.dot(jnp.concatenate(chosen, axis=1), p3[...], preferred_element_type=F32)
        grouped = three[:, 0:128] + three[:, 128:256] + three[:, 256:384]
        coup[...] += lax.dot_general(
            grouped, tabv[t], NT_DIMS, precision=HIGHEST, preferred_element_type=F32
        )
        return carry

    lax.fori_loop(0, 8, kind_step, 0)

    for c in deposits:
        c.wait_recv()
    row_id = jnp.broadcast_to(jnp.where(valid, ident, -1)[0:1, :], (64, 128))
    sub64 = iota((64, 128), 0)
    hits_own = jnp.where(row_id == r * 64 + sub64, 1.0, 0.0).astype(F32)[:, 0:32]
    hits_far = jnp.where(jnp.broadcast_to(asked[0:1, :], (64, 128)) == r * 64 + 1 + sub64, 1.0, 0.0).astype(F32)
    far = jnp.concatenate([sd[:, c].reshape(nr * SLOTS, 128) for c in range(4)], axis=1)
    sources = hdot(hits_own, by_comp) + hdot(hits_far, far)
    for q in range(4):
        rows = slice(16 * q, 16 * q + 16)
        lanes = slice(128 * q, 128 * q + 128)
        for c in range(3):
            gasov[c, :, lanes] = gasv[c, :, lanes] + sources[rows, 128 * c : 128 * c + 128]
        liqv[:, lanes] = sources[rows, 384:512]
    outs = [pltpu.make_async_copy(gasov, gas_o, osem.at[1]), pltpu.make_async_copy(liqv, liq_o, osem.at[2])]
    for c in outs:
        c.start()

    @pl.when(has_prev)
    def _():
        to(pres.at[8:16], halo.at[0], ha_s.at[0], ha_r.at[0], ax=a - 1).wait_recv()

    @pl.when(has_next)
    def _():
        to(pres.at[0:8], halo.at[1], ha_s.at[1], ha_r.at[1], ax=a + 1).wait_recv()

    mine = slab[r]
    above = jnp.concatenate([halo[0, 7:8, :], mine[0:15]], axis=0)
    below = jnp.concatenate([mine[1:16], halo[1, 0:1, :]], axis=0)
    image = 6.0 * mine - below - above
    for q in range(4):
        lanes = slice(128 * q, 128 * q + 128)
        pimv[:, lanes] = image[:, lanes] + coup[pl.ds(q, 16, stride=4), :]
    outs.append(pltpu.make_async_copy(pimv, pim_o, osem.at[3]))
    outs[-1].start()

    for i in range(4):

        @pl.when(comes_from[i])
        def _(i=i):
            crossing(i).wait_recv()

    for i in range(2):
        for f in range(7):
            arrav[0, 0, f, i : i + 1, :] = xa[i, f : f + 1, 0:64]
            arrrv[0, 0, f, i : i + 1, :] = xr[i, f : f + 1, 0:32]
    outs.append(pltpu.make_async_copy(arrav, arra_o, osem.at[4]))
    outs.append(pltpu.make_async_copy(arrrv, arrr_o, osem.at[5]))
    outs[-2].start()
    outs[-1].start()

    for c in requests + replies + shares + deposits:
        c.wait_send()

    @pl.when(has_next)
    def _():
        halo_next().wait_send()

    @pl.when(has_prev)
    def _():
        halo_prev().wait_send()

    for i in range(4):

        @pl.when(sends_to[i])
        def _(i=i):
            crossing(i).wait_send()

    out_motion.wait()
    for c in outs:
        c.wait()


def out_kernel(*refs):
    sources, targets, sem = refs[:6], refs[6:12], refs[12]
    copies = [pltpu.make_async_copy(s, t, sem.at[i]) for i, (s, t) in enumerate(zip(sources, targets))]
    for c in copies:
        c.start()
    for c in copies:
        c.wait()


def on_device(na, nr, pm, ps, pb, po, gas, pres, cols, kinds, table, sa, sr, sc):
    outs = (
        jax.ShapeDtypeStruct((6, 2048), F32),
        jax.ShapeDtypeStruct((1, 1, 7, 2, 64), F32),
        jax.ShapeDtypeStruct((1, 1, 7, 2, 32), F32),
        jax.ShapeDtypeStruct((3, 16, 512), F32),
        jax.ShapeDtypeStruct((16, 512), F32),
        jax.ShapeDtypeStruct((16, 512), F32),
    )
    V = pltpu.VMEM
    dma = pltpu.SemaphoreType.DMA
    anyspec = pl.BlockSpec(memory_space=pltpu.HBM)
    scratch = [
        V((6, 2048), F32),
        V((16, 128), F32),
        V((1, 32), I32),
        V((16, 128), I32),
        V((3, 16, 512), F32),
        V((1, 4, 64), I32),
        V((1, 4, 64), I32),
        V((8, 128, 128), F32),
        V((1, 1, 2, 64), I32),
        V((1, 1, 2, 32), I32),
        V((1, 1, 4), I32),
        V((nr, 16, 512), F32),
        V((8, 128), I32),
        V((nr, 16, 128), I32),
        V((16, 128), I32),
        V((nr, 3, 8, 128), F32),
        V((nr, 3, 8, 128), F32),
        V((8, 2048), F32),
        V((3, 16, 128), F32),
        V((32, 8, 128), F32),
        V((nr, 4, SLOTS, 128), F32),
        V((4, SLOTS, 128), F32),
        V((2, 8, 512), F32),
        V((4, 8, 128), F32),
        V((2, 8, 128), F32),
        V((2, 8, 128), F32),
        V((4, 64, 128), I32),
        V((64, 128), F32),
        V((512, 384), BF16),
        V((6, 2048), F32),
        V((1, 1, 7, 2, 64), F32),
        V((1, 1, 7, 2, 32), F32),
        V((3, 16, 512), F32),
        V((16, 512), F32),
        V((16, 512), F32),
        dma((12,)),
        dma((6,)),
        dma((8,)),
        dma((8,)),
        dma((8,)),
        dma((8,)),
        dma((8,)),
        dma((8,)),
        dma((8,)),
        dma((8,)),
        dma((2,)),
        dma((2,)),
        dma((4,)),
        dma((4,)),
    ]
    parts = pl.pallas_call(
        functools.partial(step_kernel, na, nr),
        out_shape=outs,
        in_specs=[anyspec] * 12,
        out_specs=[anyspec] * 6,
        scratch_shapes=scratch,
        compiler_params=pltpu.CompilerParams(
            collective_id=0, has_side_effects=True, vmem_limit_bytes=VMEM_BYTES
        ),
        name="step",
    )(
        pm,
        ps.reshape(16, 128),
        pb.reshape(1, 32),
        po.reshape(16, 128),
        gas,
        pres,
        jnp.swapaxes(cols, 1, 2),
        jnp.swapaxes(kinds, 1, 2),
        table,
        sa,
        sr,
        sc,
    )
    motion, axial, radial, gas_out, load, image = pl.pallas_call(
        out_kernel,
        out_shape=outs,
        in_specs=[anyspec] * 6,
        out_specs=[anyspec] * 6,
        scratch_shapes=[dma((6,))],
        compiler_params=pltpu.CompilerParams(vmem_limit_bytes=VMEM_BYTES),
        name="copy_out",
    )(*parts)
    return motion, jnp.swapaxes(axial, 2, 3), jnp.swapaxes(radial, 2, 3), gas_out, load, image


def solution(mesh):
    na, nr = mesh.shape["ax"], mesh.shape["rad"]
    return jax.shard_map(
        functools.partial(on_device, na, nr),
        mesh=mesh,
        in_specs=(
            P(None, ("ax", "rad")),
            P(("ax", "rad")),
            P(("ax", "rad")),
            P(("ax", "rad")),
            P(None, "ax", "rad"),
            P("ax", "rad"),
            P("ax", "rad", None),
            P("ax", "rad", None),
            P(),
            P("ax", "rad", None, None),
            P("ax", "rad", None, None),
            P("ax", "rad", None),
        ),
        out_specs=(
            P(None, ("ax", "rad")),
            P("ax", "rad", None, None, None),
            P("ax", "rad", None, None, None),
            P(None, "ax", "rad"),
            P("ax", "rad"),
            P("ax", "rad"),
        ),
        check_vma=False,
    )
```

```python
import functools

import jax
import jax.numpy as jnp
from jax import lax
from jax.experimental import pallas as pl
from jax.experimental.pallas import tpu as pltpu
from jax.sharding import PartitionSpec as P

MESH = pl.DeviceIdType.MESH
F32 = jnp.float32
BF16 = jnp.bfloat16
I32 = jnp.int32
HIGHEST = lax.Precision.HIGHEST
SLOTS = 16
ROWS = 5
VMEM_BYTES = 62 * 1024 * 1024
NT_DIMS = (((1,), (1,)), ((), ()))


def hdot(a, b):
    return jnp.dot(a, b, precision=HIGHEST, preferred_element_type=F32)


def split3(x):
    hi = x.astype(BF16)
    rest = x - hi.astype(F32)
    mid = rest.astype(BF16)
    lo = (rest - mid.astype(F32)).astype(BF16)
    return hi, mid, lo


def pieces(x):
    return jnp.concatenate(split3(x), axis=0)


def pick(onehot, x3):
    return jnp.dot(onehot.astype(BF16), x3, preferred_element_type=F32)


def iota(shape, dim):
    return lax.broadcasted_iota(I32, shape, dim)


def lane_gather(x, index):
    return jnp.take_along_axis(x, index, axis=1)


def step_kernel(
    na,
    nr,
    pm,
    ps,
    pb,
    po,
    gas,
    pres,
    cols,
    kinds,
    table,
    sa,
    sr,
    sc,
    motv,
    arrav,
    arrrv,
    gasov,
    liqv,
    pimv,
    pmv,
    psv,
    pbv,
    pov,
    gasv,
    colv,
    kindv,
    tabv,
    sav,
    srv,
    scv,
    slab,
    rows8,
    rq,
    rqs,
    rp,
    rps,
    uown,
    dp,
    sd,
    sds,
    halo,
    xs,
    xa,
    xr,
    keys,
    coup,
    p3,
    lsem,
    rq_s,
    rq_r,
    rp_s,
    rp_r,
    pr_s,
    pr_r,
    sd_s,
    sd_r,
    ha_s,
    ha_r,
    x_s,
    x_r,
):
    a = lax.axis_index("ax")
    r = lax.axis_index("rad")
    has_prev, has_next = a > 0, a < na - 1
    has_in, has_out = r > 0, r < nr - 1

    def to(src, dst, ssem, rsem, **where):
        return pltpu.make_async_remote_copy(
            src_ref=src, dst_ref=dst, send_sem=ssem, recv_sem=rsem, device_id=where, device_id_type=MESH
        )

    barrier = pltpu.get_barrier_semaphore()
    for k in range(1, nr):
        pl.semaphore_signal(barrier, inc=1, device_id={"rad": lax.rem(r + k, nr)}, device_id_type=MESH)

    @pl.when(has_prev)
    def _():
        pl.semaphore_signal(barrier, inc=1, device_id={"ax": a - 1}, device_id_type=MESH)

    @pl.when(has_next)
    def _():
        pl.semaphore_signal(barrier, inc=1, device_id={"ax": a + 1}, device_id_type=MESH)

    loads = [
        pltpu.make_async_copy(src, dst, lsem.at[i])
        for i, (src, dst) in enumerate(
            (
                (pb, pbv),
                (po, pov),
                (gas, gasv),
                (ps, psv),
                (pm, pmv),
                (sa, sav),
                (sr, srv),
                (sc, scv),
                (pres, slab.at[r]),
                (cols, colv),
                (kinds, kindv),
                (table, tabv),
            )
        )
    ]
    for load in loads:
        load.start()

    lane8 = iota((8, 128), 1)
    sub8 = iota((8, 128), 0)
    lane16 = iota((16, 128), 1)
    low8 = lane8 < 64
    low16 = lane16 < 64

    rows8[...] = jnp.zeros((8, 128), I32)
    loads[0].wait()
    loads[1].wait()
    rows8[0:1, 0:32] = pbv[...]
    blocks = jnp.broadcast_to(rows8[0:1, :], (8, 128))
    order = jnp.bitwise_and(jnp.where(lane8 < 16, 2 * lane8, 2 * lane8 - 31), 127)
    blocks = lane_gather(blocks, order)
    owner = jnp.right_shift(blocks, 6)
    local = jnp.bitwise_and(blocks, 63)
    ident = owner * 64 + jnp.bitwise_and(local, 3) * 16 + jnp.right_shift(local, 2)
    valid = lane8 < 32

    def thrice(x):
        return jnp.where(lane8 < 32, x, jnp.where(lane8 < 64, pltpu.roll(x, 32, axis=1), pltpu.roll(x, 64, axis=1)))

    away = jnp.where(valid & (owner != r), 1, 0)
    rank = away
    for s in (1, 2, 4, 8, 16):
        rank = rank + jnp.where(lane8 >= s, pltpu.roll(rank, s, axis=1), 0)
    rank = rank - away
    row_rank = jnp.where(away > 0, rank, -1)
    code = jnp.where(valid, (rank * 2 + away) * 1024 + ident, 0)
    col = jnp.transpose(jnp.broadcast_to(code[0:1, :], (128, 128)))[0:32, :]
    col_id = jnp.bitwise_and(col, 1023)
    col_away = jnp.bitwise_and(jnp.right_shift(col, 10), 1)
    col_rank = jnp.right_shift(col, 11)
    lane32 = iota((32, 128), 1)
    picked = jnp.where((col_away > 0) & (col_rank + SLOTS * r == lane32), col_id + 1, 0)
    ids = picked[0:8] + picked[8:16] + picked[16:24] + picked[24:32]
    for s in (4, 2, 1):
        ids = ids + pltpu.roll(ids, s, axis=0)
    to_slot = jnp.where(
        jnp.broadcast_to(row_rank[0:1, :], (SLOTS, 128)) == iota((SLOTS, 128), 0), 1.0, 0.0
    ).astype(F32)[:, 0:32]
    offsets = pov[...]
    offs_f = offsets.astype(F32)
    slot_offs = jnp.dot(
        to_slot.astype(BF16),
        jnp.concatenate([offs_f, pltpu.roll(offs_f, 64, axis=1)], axis=0).astype(BF16),
        preferred_element_type=F32,
    ).astype(I32)
    rqs[0:8, :] = jnp.where(low8, slot_offs[0:8], pltpu.roll(slot_offs[8:16], 64, axis=1))
    rqs[8:9, :] = ids[0:1]

    rq[r] = jnp.zeros((16, 128), I32)
    rp[r] = jnp.zeros((3, 8, 128), F32)
    sd[r] = jnp.zeros((ROWS, SLOTS, 128), F32)

    @pl.when(jnp.logical_not(has_prev))
    def _():
        xa[0] = jnp.zeros((8, 128), F32)
        halo[0] = jnp.zeros((8, 512), F32)

    @pl.when(jnp.logical_not(has_next))
    def _():
        xa[1] = jnp.zeros((8, 128), F32)
        halo[1] = jnp.zeros((8, 512), F32)

    @pl.when(jnp.logical_not(has_in))
    def _():
        xr[0] = jnp.zeros((8, 128), F32)

    @pl.when(jnp.logical_not(has_out))
    def _():
        xr[1] = jnp.zeros((8, 128), F32)

    pl.semaphore_wait(barrier, nr - 1 + has_prev.astype(I32) + has_next.astype(I32))

    core = lax.rem(r, 2)
    sibling = r + 1 - 2 * core

    def spread_out(src, dst, ssem, rsem):
        copies = []
        for j in range(4):
            target = lax.rem(r + 2 * j, nr) if j else sibling
            c = to(src, dst.at[r], ssem.at[j], rsem.at[j], rad=target)
            c.start()
            copies.append(c)
        return copies

    def pass_on(copies, dst, ssem, rsem):
        again = []
        for j in range(1, 4):
            copies[j].wait_recv()
            origin = dst.at[lax.rem(r + nr - 2 * j, nr)]
            c = to(origin, origin, ssem.at[3 + j], rsem.at[3 + j], rad=sibling)
            c.start()
            again.append(c)
        return again

    requests = []
    for k in range(1, nr):
        c = to(rqs.at[0:9], rq.at[r, 0:9], rq_s.at[k], rq_r.at[k], rad=lax.rem(r + k, nr))
        c.start()
        requests.append(c)

    shares = spread_out(pres, slab, pr_s, pr_r)

    def halo_next():
        return to(pres.at[8:16], halo.at[0], ha_s.at[0], ha_r.at[0], ax=a + 1)

    def halo_prev():
        return to(pres.at[0:8], halo.at[1], ha_s.at[1], ha_r.at[1], ax=a - 1)

    @pl.when(has_next)
    def _():
        halo_next().start()

    @pl.when(has_prev)
    def _():
        halo_prev().start()

    loads[2].wait()
    gas_rows = jnp.concatenate(
        [
            jnp.concatenate([gasv[c, :, 128 * q : 128 * q + 128] for q in range(4)], axis=0)
            for c in range(3)
        ],
        axis=1,
    )
    gas3 = pieces(gas_rows)
    at_own = jnp.where(col_id[:, 0:1] == r * 64 + jnp.bitwise_and(iota((32, 192), 1), 63), 1.0, 0.0)
    found = pick(at_own, gas3)
    for c in range(3):
        part = found[:, 128 * c : 128 * c + 128]
        uown[c] = jnp.where(low16, lane_gather(part[0:16], offsets), lane_gather(part[16:32], offsets))

    loads[3].wait()
    size = psv[...]
    factor = jnp.exp(-0.5 / (size * size))
    mass = size * size * size
    share = mass * (1.0 - factor)
    loads[4].wait()
    is_vel = (sub8 >= 3) & (sub8 < 6)
    sub128 = iota((128, 128), 0)
    for t in range(16):
        row = lambda x: jnp.broadcast_to(x[t : t + 1, :], (8, 128))
        old = jnp.concatenate([pmv[:, 128 * t : 128 * t + 128], jnp.zeros((2, 128), F32)], axis=0)
        d = row(share) * jnp.where(is_vel, old, 1.0)
        d = jnp.where(sub8 == 6, row(mass), d)
        both = jnp.concatenate([jnp.where(low8, d, 0.0), jnp.where(low8, 0.0, d)], axis=0)
        cells = jnp.where(jnp.broadcast_to(offsets[t : t + 1, :], (128, 128)) == sub128, 1.0, 0.0).astype(BF16)
        sums = lax.dot_general(pieces(both), cells, NT_DIMS, preferred_element_type=F32)
        sums = sums[0:16] + sums[16:32] + sums[32:48]
        dp[t] = sums[0:8]
        dp[16 + t] = sums[8:16]
    own3 = pieces(jnp.concatenate([dp[:, 2 + c, :] for c in range(ROWS)], axis=1))
    slot_of = jnp.broadcast_to(thrice(row_rank)[0:1, 0:96], (SLOTS, 96))
    slotted = pick(jnp.where(slot_of == iota((SLOTS, 96), 0), 1.0, 0.0), own3)
    for c in range(ROWS):
        sds[c] = slotted[:, 128 * c : 128 * c + 128]

    for c in requests:
        c.wait_recv()
    asked = rq[0, 8:9, :]
    for s in range(1, nr):
        asked = asked + rq[s, 8:9, :]
    asked_col = jnp.transpose(jnp.broadcast_to(asked[0:1, :], (128, 128)))
    at_asked = jnp.where(asked_col[:, 0:1] == r * 64 + 1 + jnp.bitwise_and(iota((128, 192), 1), 63), 1.0, 0.0)
    found = pick(at_asked, gas3)
    for s in range(nr):
        index = rq[s, 0:8, :]
        for c in range(3):
            part = found[SLOTS * s : SLOTS * s + 16, 128 * c : 128 * c + 128]
            rps[s, c] = jnp.where(low8, lane_gather(part[0:8], index), lane_gather(part[8:16], index))
    replies = []
    for k in range(1, nr):
        dst = lax.rem(r + k, nr)
        c = to(rps.at[dst], rp.at[r], rp_s.at[k], rp_r.at[k], rad=dst)
        c.start()
        replies.append(c)
    deposits = spread_out(sds, sd, sd_s, sd_r)
    share_again = pass_on(shares, slab, pr_s, pr_r)

    loads[9].wait()
    loads[10].wait()
    cv = colv[0]
    key = kindv[0] * 512 + jnp.bitwise_and(cv, 3) * 128 + jnp.right_shift(cv, 6) * 16
    key = key + jnp.bitwise_and(jnp.right_shift(cv, 2), 15)
    rows8[4:8, 0:64] = key
    for k in range(4):
        keys[k] = jnp.transpose(jnp.broadcast_to(rows8[4 + k : 5 + k, :], (128, 128)))[0:64, :]

    for i in (5, 6, 7):
        loads[i].wait()
    rows8[0:2, 0:64] = sav[0, 0]
    rows8[2:4, 0:32] = srv[0, 0]
    lists = [jnp.broadcast_to(rows8[i : i + 1, :], (8, 128)) for i in range(4)]
    counts = [jnp.broadcast_to(scv[0, :, i : i + 1], (8, 128)) for i in range(4)]
    list_ax = jnp.where(low8, lists[0], pltpu.roll(lists[1], 64, axis=1))
    list_rad = jnp.where(low8, lists[2], pltpu.roll(lists[3], 64, axis=1))
    live_ax = lane8 < jnp.where(low8, counts[0], counts[1] + 64)
    live_rad = lane8 < jnp.where(low8, counts[2], counts[3] + 64)

    seat = jnp.where(col_away > 0, jnp.right_shift(col_id, 6) * 8 + jnp.bitwise_and(col_rank, 7), -1)
    seat = jnp.concatenate([jnp.where(col_rank < 8, seat, -1), jnp.where(col_rank < 8, -1, seat)], axis=0)
    w = jnp.where(seat[:, 0:1] == jnp.bitwise_and(iota((64, 192), 1), 63), 1.0, 0.0)

    for c in replies:
        c.wait_recv()
    answer = jnp.concatenate([rp[:, c].reshape(nr * 8, 128) for c in range(3)], axis=1)
    spread = pick(w, pieces(answer))
    u = []
    for c in range(3):
        lo, hi = spread[0:32, 128 * c : 128 * c + 128], spread[32:64, 128 * c : 128 * c + 128]
        even = lo[0:16] + pltpu.roll(hi[0:16], 64, axis=1)
        odd = pltpu.roll(lo[16:32], 64, axis=1) + hi[16:32]
        u.append(uown[c] + jnp.where(low16, even, odd))

    cross_ax = jnp.zeros((8, 128), F32)
    cross_rad = jnp.zeros((8, 128), F32)
    tile_ax, lane_ax = jnp.right_shift(list_ax, 7), jnp.bitwise_and(list_ax, 127)
    tile_rad, lane_rad = jnp.right_shift(list_rad, 7), jnp.bitwise_and(list_rad, 127)
    for t in range(16):
        row = lambda x: jnp.broadcast_to(x[t : t + 1, :], (8, 128))
        old = jnp.concatenate([pmv[:, 128 * t : 128 * t + 128], jnp.zeros((2, 128), F32)], axis=0)
        gas_t = jnp.where(sub8 == 3, row(u[0]), jnp.where(sub8 == 4, row(u[1]), row(u[2])))
        vel = gas_t + (old - gas_t) * row(factor)
        pos = old + 0.5 * pltpu.roll(vel, 5, axis=0)
        new = jnp.where(sub8 < 3, pos, jnp.where(is_vel, vel, row(size)))
        motv[:, 128 * t : 128 * t + 128] = new[0:6]
        cross_ax = jnp.where(tile_ax == t, lane_gather(new, lane_ax), cross_ax)
        cross_rad = jnp.where(tile_rad == t, lane_gather(new, lane_rad), cross_rad)
    cross_ax = jnp.where(live_ax, cross_ax, 0.0)
    cross_rad = jnp.where(live_rad, cross_rad, 0.0)
    xs[0] = cross_ax
    xs[1] = pltpu.roll(cross_ax, 64, axis=1)
    xs[2] = cross_rad
    xs[3] = pltpu.roll(cross_rad, 64, axis=1)

    def crossing(i):
        dst = (xa.at[0], xa.at[1], xr.at[0], xr.at[1])[i]
        where = ({"ax": a + 1}, {"ax": a - 1}, {"rad": r + 1}, {"rad": r - 1})[i]
        return to(xs.at[i], dst, x_s.at[i], x_r.at[i], **where)

    sends_to = (has_next, has_prev, has_out, has_in)
    comes_from = (has_prev, has_next, has_in, has_out)
    for i in range(4):

        @pl.when(sends_to[i])
        def _(i=i):
            crossing(i).start()

    loads[8].wait()
    loads[11].wait()
    deposit_again = pass_on(deposits, sd, sd_s, sd_r)
    for c in shares[:1] + share_again:
        c.wait_recv()
    slab_rows = jnp.concatenate(
        [slab[:, :, 128 * q : 128 * q + 128].reshape(nr * 16, 128) for q in range(4)], axis=0
    )
    p3[...] = jnp.concatenate(split3(slab_rows), axis=1)
    coup[...] = jnp.zeros((64, 128), F32)
    lane64 = iota((64, 128), 1)

    def kind_step(t, carry):
        chosen = []
        for q in range(4):
            want = t * 512 + q * 128 + lane64
            g = jnp.where(keys[0] == want, 1.0, 0.0)
            for k in range(1, 4):
                g = g + jnp.where(keys[k] == want, 1.0, 0.0)
            chosen.append(g.astype(BF16))
        three = jnp.dot(jnp.concatenate(chosen, axis=1), p3[...], preferred_element_type=F32)
        grouped = three[:, 0:128] + three[:, 128:256] + three[:, 256:384]
        coup[...] += lax.dot_general(
            grouped, tabv[t], NT_DIMS, precision=HIGHEST, preferred_element_type=F32
        )
        return carry

    lax.fori_loop(0, 8, kind_step, 0)

    for c in deposits[:1] + deposit_again:
        c.wait_recv()
    own_at = jnp.broadcast_to(thrice(ident)[0:1, 0:96], (64, 96))
    far_at = jnp.broadcast_to(jnp.concatenate([asked] * 3, axis=1), (64, 384))
    hits_own = jnp.where(own_at == r * 64 + iota((64, 96), 0), 1.0, 0.0)
    hits_far = jnp.where(far_at == r * 64 + 1 + iota((64, 384), 0), 1.0, 0.0)
    far = jnp.concatenate([sd[:, c].reshape(nr * SLOTS, 128) for c in range(ROWS)], axis=1)
    sources = pick(hits_own, own3) + pick(hits_far, pieces(far))
    for q in range(4):
        rows = slice(16 * q, 16 * q + 16)
        lanes = slice(128 * q, 128 * q + 128)
        weight = sources[rows, 0:128]
        for c in range(3):
            g = gasv[c, :, lanes]
            gasov[c, :, lanes] = g + (sources[rows, 128 * c + 128 : 128 * c + 256] - g * weight)
        liqv[:, lanes] = sources[rows, 512:640]

    @pl.when(has_prev)
    def _():
        to(pres.at[8:16], halo.at[0], ha_s.at[0], ha_r.at[0], ax=a - 1).wait_recv()

    @pl.when(has_next)
    def _():
        to(pres.at[0:8], halo.at[1], ha_s.at[1], ha_r.at[1], ax=a + 1).wait_recv()

    mine = slab[r]
    above = jnp.concatenate([halo[0, 7:8, :], mine[0:15]], axis=0)
    below = jnp.concatenate([mine[1:16], halo[1, 0:1, :]], axis=0)
    image = 6.0 * mine - below - above
    for q in range(4):
        lanes = slice(128 * q, 128 * q + 128)
        pimv[:, lanes] = image[:, lanes] + coup[pl.ds(q, 16, stride=4), :]

    for i in range(4):

        @pl.when(comes_from[i])
        def _(i=i):
            crossing(i).wait_recv()

    for i in range(2):
        for f in range(7):
            arrav[0, 0, f, i : i + 1, :] = xa[i, f : f + 1, 0:64]
            arrrv[0, 0, f, i : i + 1, :] = xr[i, f : f + 1, 0:32]
    for c in requests + replies + shares + deposits + share_again + deposit_again:
        c.wait_send()

    @pl.when(has_next)
    def _():
        halo_next().wait_send()

    @pl.when(has_prev)
    def _():
        halo_prev().wait_send()

    for i in range(4):

        @pl.when(sends_to[i])
        def _(i=i):
            crossing(i).wait_send()


def out_kernel(*refs):
    sources, targets, sem = refs[:6], refs[6:12], refs[12]
    copies = [pltpu.make_async_copy(s, t, sem.at[i]) for i, (s, t) in enumerate(zip(sources, targets))]
    for c in copies:
        c.start()
    for c in copies:
        c.wait()


def on_device(na, nr, pm, ps, pb, po, gas, pres, cols, kinds, table, sa, sr, sc):
    outs = (
        jax.ShapeDtypeStruct((6, 2048), F32),
        jax.ShapeDtypeStruct((1, 1, 7, 2, 64), F32),
        jax.ShapeDtypeStruct((1, 1, 7, 2, 32), F32),
        jax.ShapeDtypeStruct((3, 16, 512), F32),
        jax.ShapeDtypeStruct((16, 512), F32),
        jax.ShapeDtypeStruct((16, 512), F32),
    )
    V = pltpu.VMEM
    dma = pltpu.SemaphoreType.DMA
    anyspec = pl.BlockSpec(memory_space=pltpu.HBM)
    scratch = [
        V((6, 2048), F32),
        V((16, 128), F32),
        V((1, 32), I32),
        V((16, 128), I32),
        V((3, 16, 512), F32),
        V((1, 4, 64), I32),
        V((1, 4, 64), I32),
        V((8, 128, 128), F32),
        V((1, 1, 2, 64), I32),
        V((1, 1, 2, 32), I32),
        V((1, 1, 4), I32),
        V((nr, 16, 512), F32),
        V((8, 128), I32),
        V((nr, 16, 128), I32),
        V((16, 128), I32),
        V((nr, 3, 8, 128), F32),
        V((nr, 3, 8, 128), F32),
        V((3, 16, 128), F32),
        V((32, 8, 128), F32),
        V((nr, ROWS, SLOTS, 128), F32),
        V((ROWS, SLOTS, 128), F32),
        V((2, 8, 512), F32),
        V((4, 8, 128), F32),
        V((2, 8, 128), F32),
        V((2, 8, 128), F32),
        V((4, 64, 128), I32),
        V((64, 128), F32),
        V((512, 384), BF16),
        dma((12,)),
        dma((8,)),
        dma((8,)),
        dma((8,)),
        dma((8,)),
        dma((8,)),
        dma((8,)),
        dma((8,)),
        dma((8,)),
        dma((2,)),
        dma((2,)),
        dma((4,)),
        dma((4,)),
    ]
    parts = pl.pallas_call(
        functools.partial(step_kernel, na, nr),
        out_shape=[pltpu.VMEM(o.shape, o.dtype) for o in outs],
        in_specs=[anyspec] * 12,
        out_specs=[pl.BlockSpec(memory_space=pltpu.VMEM)] * 6,
        scratch_shapes=scratch,
        compiler_params=pltpu.CompilerParams(
            collective_id=0, has_side_effects=True, vmem_limit_bytes=VMEM_BYTES
        ),
        name="step",
    )(
        pm,
        ps.reshape(16, 128),
        pb.reshape(1, 32),
        po.reshape(16, 128),
        gas,
        pres,
        jnp.swapaxes(cols, 1, 2),
        jnp.swapaxes(kinds, 1, 2),
        table,
        sa,
        sr,
        sc,
    )
    motion, axial, radial, gas_out, load, image = pl.pallas_call(
        out_kernel,
        out_shape=outs,
        in_specs=[pl.BlockSpec(memory_space=pltpu.VMEM)] * 6,
        out_specs=[anyspec] * 6,
        scratch_shapes=[dma((6,))],
        compiler_params=pltpu.CompilerParams(vmem_limit_bytes=1024 * 1024),
        name="copy_out",
    )(*parts)
    return motion, jnp.swapaxes(axial, 2, 3), jnp.swapaxes(radial, 2, 3), gas_out, load, image


def solution(mesh):
    na, nr = mesh.shape["ax"], mesh.shape["rad"]
    return jax.shard_map(
        functools.partial(on_device, na, nr),
        mesh=mesh,
        in_specs=(
            P(None, ("ax", "rad")),
            P(("ax", "rad")),
            P(("ax", "rad")),
            P(("ax", "rad")),
            P(None, "ax", "rad"),
            P("ax", "rad"),
            P("ax", "rad", None),
            P("ax", "rad", None),
            P(),
            P("ax", "rad", None, None),
            P("ax", "rad", None, None),
            P("ax", "rad", None),
        ),
        out_specs=(
            P(None, ("ax", "rad")),
            P("ax", "rad", None, None, None),
            P("ax", "rad", None, None, None),
            P(None, "ax", "rad"),
            P("ax", "rad"),
            P("ax", "rad"),
        ),
        check_vma=False,
    )
```

```python
import functools

import jax
import jax.numpy as jnp
from jax import lax
from jax.experimental import pallas as pl
from jax.experimental.pallas import tpu as pltpu
from jax.sharding import PartitionSpec as P

MESH = pl.DeviceIdType.MESH
F32 = jnp.float32
BF16 = jnp.bfloat16
I32 = jnp.int32
HIGHEST = lax.Precision.HIGHEST
SLOTS = 16
ROWS = 5
VMEM_BYTES = 62 * 1024 * 1024
NT_DIMS = (((1,), (1,)), ((), ()))


def hdot(a, b):
    return jnp.dot(a, b, precision=HIGHEST, preferred_element_type=F32)


def split3(x):
    hi = x.astype(BF16)
    rest = x - hi.astype(F32)
    mid = rest.astype(BF16)
    lo = (rest - mid.astype(F32)).astype(BF16)
    return hi, mid, lo


def pieces(x):
    return jnp.concatenate(split3(x), axis=0)


def pick(onehot, x3):
    return jnp.dot(onehot.astype(BF16), x3, preferred_element_type=F32)


def iota(shape, dim):
    return lax.broadcasted_iota(I32, shape, dim)


def lane_gather(x, index):
    return jnp.take_along_axis(x, index, axis=1)


def step_kernel(
    na,
    nr,
    pm,
    ps,
    pb,
    po,
    gas,
    pres,
    cols,
    kinds,
    table,
    sa,
    sr,
    sc,
    motv,
    arrav,
    arrrv,
    gasov,
    liqv,
    pimv,
    pmv,
    psv,
    pbv,
    pov,
    gasv,
    colv,
    kindv,
    tabv,
    sav,
    srv,
    scv,
    slab,
    rows8,
    rq,
    rqs,
    rp,
    rps,
    uown,
    dp,
    sd,
    sds,
    halo,
    xs,
    xa,
    xr,
    keys,
    coup,
    p3,
    chosen,
    tab3,
    lsem,
    rq_s,
    rq_r,
    rp_s,
    rp_r,
    pr_s,
    pr_r,
    sd_s,
    sd_r,
    ha_s,
    ha_r,
    x_s,
    x_r,
    slab_go,
    ax_go,
):
    a = lax.axis_index("ax")
    r = lax.axis_index("rad")
    has_prev, has_next = a > 0, a < na - 1
    has_in, has_out = r > 0, r < nr - 1

    def to(src, dst, ssem, rsem, **where):
        return pltpu.make_async_remote_copy(
            src_ref=src, dst_ref=dst, send_sem=ssem, recv_sem=rsem, device_id=where, device_id_type=MESH
        )

    core = lax.rem(r, 2)
    sibling = r + 1 - 2 * core
    barrier = pltpu.get_barrier_semaphore()
    for k in range(1, 4):
        even = lax.rem(r - core + 2 * k, nr)
        pl.semaphore_signal(barrier, inc=1, device_id={"rad": even}, device_id_type=MESH)

    @pl.when(core == 1)
    def _():
        pl.semaphore_signal(barrier, inc=1, device_id={"rad": sibling}, device_id_type=MESH)

    @pl.when(has_prev)
    def _():
        pl.semaphore_signal(barrier, inc=1, device_id={"ax": a - 1, "rad": r - core + 1}, device_id_type=MESH)

    @pl.when(has_next)
    def _():
        pl.semaphore_signal(barrier, inc=1, device_id={"ax": a + 1, "rad": r - core + 1}, device_id_type=MESH)

    loads = [
        pltpu.make_async_copy(src, dst, lsem.at[i])
        for i, (src, dst) in enumerate(
            (
                (pb, pbv),
                (po, pov),
                (gas, gasv),
                (ps, psv),
                (pm, pmv),
                (sa, sav),
                (sr, srv),
                (sc, scv),
                (pres, slab.at[r]),
                (cols, colv),
                (kinds, kindv),
                (table, tabv),
            )
        )
    ]
    for load in loads:
        load.start()

    lane8 = iota((8, 128), 1)
    sub8 = iota((8, 128), 0)
    lane16 = iota((16, 128), 1)
    low8 = lane8 < 64
    low16 = lane16 < 64

    rows8[...] = jnp.zeros((8, 128), I32)
    loads[0].wait()
    loads[1].wait()
    rows8[0:1, 0:32] = pbv[...]
    blocks = jnp.broadcast_to(rows8[0:1, :], (8, 128))
    order = jnp.bitwise_and(jnp.where(lane8 < 16, 2 * lane8, 2 * lane8 - 31), 127)
    blocks = lane_gather(blocks, order)
    owner = jnp.right_shift(blocks, 6)
    local = jnp.bitwise_and(blocks, 63)
    ident = owner * 64 + jnp.bitwise_and(local, 3) * 16 + jnp.right_shift(local, 2)
    valid = lane8 < 32

    def thrice(x):
        return jnp.where(lane8 < 32, x, jnp.where(lane8 < 64, pltpu.roll(x, 32, axis=1), pltpu.roll(x, 64, axis=1)))

    away = jnp.where(valid & (owner != r), 1, 0)
    rank = away
    for s in (1, 2, 4, 8, 16):
        rank = rank + jnp.where(lane8 >= s, pltpu.roll(rank, s, axis=1), 0)
    rank = rank - away
    row_rank = jnp.where(away > 0, rank, -1)
    code = jnp.where(valid, (rank * 2 + away) * 1024 + ident, 0)
    col = jnp.transpose(jnp.broadcast_to(code[0:1, :], (128, 128)))[0:32, :]
    col_id = jnp.bitwise_and(col, 1023)
    col_away = jnp.bitwise_and(jnp.right_shift(col, 10), 1)
    col_rank = jnp.right_shift(col, 11)
    lane32 = iota((32, 128), 1)
    picked = jnp.where((col_away > 0) & (col_rank + SLOTS * r == lane32), col_id + 1, 0)
    ids = picked[0:8] + picked[8:16] + picked[16:24] + picked[24:32]
    for s in (4, 2, 1):
        ids = ids + pltpu.roll(ids, s, axis=0)
    to_slot = jnp.where(
        jnp.broadcast_to(row_rank[0:1, :], (SLOTS, 128)) == iota((SLOTS, 128), 0), 1.0, 0.0
    ).astype(F32)[:, 0:32]
    offsets = pov[...]
    offs_f = offsets.astype(F32)
    slot_offs = jnp.dot(
        to_slot.astype(BF16),
        jnp.concatenate([offs_f, pltpu.roll(offs_f, 64, axis=1)], axis=0).astype(BF16),
        preferred_element_type=F32,
    ).astype(I32)
    rqs[0:8, :] = jnp.where(low8, slot_offs[0:8], pltpu.roll(slot_offs[8:16], 64, axis=1))
    rqs[8:9, :] = ids[0:1]

    rq[r] = jnp.zeros((16, 128), I32)
    rp[r] = jnp.zeros((3, 8, 128), F32)
    sd[r] = jnp.zeros((ROWS, SLOTS, 128), F32)

    @pl.when(jnp.logical_not(has_prev))
    def _():
        xa[0] = jnp.zeros((8, 128), F32)
        halo[0] = jnp.zeros((8, 512), F32)

    @pl.when(jnp.logical_not(has_next))
    def _():
        xa[1] = jnp.zeros((8, 128), F32)
        halo[1] = jnp.zeros((8, 512), F32)

    @pl.when(jnp.logical_not(has_in))
    def _():
        xr[0] = jnp.zeros((8, 128), F32)

    @pl.when(jnp.logical_not(has_out))
    def _():
        xr[1] = jnp.zeros((8, 128), F32)

    @pl.when(core == 0)
    def _():
        pl.semaphore_wait(barrier, nr - 1)
        pl.semaphore_signal(slab_go, inc=1, device_id={"rad": sibling}, device_id_type=MESH)

    @pl.when(core == 1)
    def _():
        pl.semaphore_wait(slab_go, 1)

    def spread_out(src, dst, ssem, rsem):
        copies = []
        for j in range(4):
            target = lax.rem(r + 2 * j, nr) if j else sibling
            c = to(src, dst.at[r], ssem.at[j], rsem.at[j], rad=target)
            c.start()
            copies.append(c)
        return copies

    def pass_on(copies, dst, ssem, rsem):
        again = []
        for j in range(1, 4):
            copies[j].wait_recv()
            origin = dst.at[lax.rem(r + nr - 2 * j, nr)]
            c = to(origin, origin, ssem.at[3 + j], rsem.at[3 + j], rad=sibling)
            c.start()
            again.append(c)
        return again

    requests = []
    for k in range(1, nr):
        c = to(rqs.at[0:9], rq.at[r, 0:9], rq_s.at[k], rq_r.at[k], rad=lax.rem(r + k, nr))
        c.start()
        requests.append(c)

    shares = spread_out(pres, slab, pr_s, pr_r)

    def halo_next():
        return to(pres.at[8:16], halo.at[0], ha_s.at[0], ha_r.at[0], ax=a + 1)

    def halo_prev():
        return to(pres.at[0:8], halo.at[1], ha_s.at[1], ha_r.at[1], ax=a - 1)

    loads[2].wait()
    gas_rows = jnp.concatenate(
        [
            jnp.concatenate([gasv[c, :, 128 * q : 128 * q + 128] for q in range(4)], axis=0)
            for c in range(3)
        ],
        axis=1,
    )
    gas3 = pieces(gas_rows)
    at_own = jnp.where(col_id[:, 0:1] == r * 64 + jnp.bitwise_and(iota((32, 192), 1), 63), 1.0, 0.0)
    found = pick(at_own, gas3)
    for c in range(3):
        part = found[:, 128 * c : 128 * c + 128]
        uown[c] = jnp.where(low16, lane_gather(part[0:16], offsets), lane_gather(part[16:32], offsets))

    for c in requests:
        c.wait_recv()
    asked = rq[0, 8:9, :]
    for s in range(1, nr):
        asked = asked + rq[s, 8:9, :]
    asked_col = jnp.transpose(jnp.broadcast_to(asked[0:1, :], (128, 128)))
    at_asked = jnp.where(asked_col[:, 0:1] == r * 64 + 1 + jnp.bitwise_and(iota((128, 192), 1), 63), 1.0, 0.0)
    found = pick(at_asked, gas3)
    for s in range(nr):
        index = rq[s, 0:8, :]
        for c in range(3):
            part = found[SLOTS * s : SLOTS * s + 16, 128 * c : 128 * c + 128]
            rps[s, c] = jnp.where(low8, lane_gather(part[0:8], index), lane_gather(part[8:16], index))
    replies = []
    for k in range(1, nr):
        dst = lax.rem(r + k, nr)
        c = to(rps.at[dst], rp.at[r], rp_s.at[k], rp_r.at[k], rad=dst)
        c.start()
        replies.append(c)
    loads[3].wait()
    size = psv[...]
    factor = jnp.exp(-0.5 / (size * size))
    mass = size * size * size
    share = mass * (1.0 - factor)
    loads[4].wait()
    is_vel = (sub8 >= 3) & (sub8 < 6)
    sub128 = iota((128, 128), 0)
    for t in range(16):
        row = lambda x: jnp.broadcast_to(x[t : t + 1, :], (8, 128))
        old = jnp.concatenate([pmv[:, 128 * t : 128 * t + 128], jnp.zeros((2, 128), F32)], axis=0)
        d = row(share) * jnp.where(is_vel, old, 1.0)
        d = jnp.where(sub8 == 6, row(mass), d)
        both = jnp.concatenate([jnp.where(low8, d, 0.0), jnp.where(low8, 0.0, d)], axis=0)
        cells = jnp.where(jnp.broadcast_to(offsets[t : t + 1, :], (128, 128)) == sub128, 1.0, 0.0).astype(BF16)
        sums = lax.dot_general(pieces(both), cells, NT_DIMS, preferred_element_type=F32)
        sums = sums[0:16] + sums[16:32] + sums[32:48]
        dp[t] = sums[0:8]
        dp[16 + t] = sums[8:16]
    own3 = pieces(jnp.concatenate([dp[:, 2 + c, :] for c in range(ROWS)], axis=1))
    slot_of = jnp.broadcast_to(thrice(row_rank)[0:1, 0:96], (SLOTS, 96))
    slotted = pick(jnp.where(slot_of == iota((SLOTS, 96), 0), 1.0, 0.0), own3)
    for c in range(ROWS):
        sds[c] = slotted[:, 128 * c : 128 * c + 128]

    deposits = spread_out(sds, sd, sd_s, sd_r)
    share_again = pass_on(shares, slab, pr_s, pr_r)

    loads[9].wait()
    loads[10].wait()
    cv = colv[0]
    key = kindv[0] * 512 + jnp.bitwise_and(cv, 3) * 128 + jnp.right_shift(cv, 6) * 16
    key = key + jnp.bitwise_and(jnp.right_shift(cv, 2), 15)
    rows8[4:8, 0:64] = key
    for k in range(4):
        keys[k] = jnp.transpose(jnp.broadcast_to(rows8[4 + k : 5 + k, :], (128, 128)))[0:64, :]
    lane64 = iota((64, 128), 1)

    def choose(t, carry):
        for q in range(4):
            want = t * 512 + q * 128 + lane64
            g = jnp.where(keys[0] == want, 1.0, 0.0)
            for k in range(1, 4):
                g = g + jnp.where(keys[k] == want, 1.0, 0.0)
            chosen[pl.ds(pl.multiple_of(64 * t, 64), 64), 128 * q : 128 * q + 128] = g.astype(BF16)
        return carry

    lax.fori_loop(0, 8, choose, 0)
    loads[11].wait()
    for t in range(8):
        tab = tabv[t]
        tab_high = tab.astype(BF16)
        tab3[:, 128 * t : 128 * t + 128] = tab_high
        tab3[:, 1024 + 128 * t : 1152 + 128 * t] = tab_high
        tab3[:, 2048 + 128 * t : 2176 + 128 * t] = (tab - tab_high.astype(F32)).astype(BF16)

    for i in (5, 6, 7):
        loads[i].wait()
    rows8[0:2, 0:64] = sav[0, 0]
    rows8[2:4, 0:32] = srv[0, 0]
    lists = [jnp.broadcast_to(rows8[i : i + 1, :], (8, 128)) for i in range(4)]
    counts = [jnp.broadcast_to(scv[0, :, i : i + 1], (8, 128)) for i in range(4)]
    list_ax = jnp.where(low8, lists[0], pltpu.roll(lists[1], 64, axis=1))
    list_rad = jnp.where(low8, lists[2], pltpu.roll(lists[3], 64, axis=1))
    live_ax = lane8 < jnp.where(low8, counts[0], counts[1] + 64)
    live_rad = lane8 < jnp.where(low8, counts[2], counts[3] + 64)

    seat = jnp.where(col_away > 0, jnp.right_shift(col_id, 6) * 8 + jnp.bitwise_and(col_rank, 7), -1)
    seat = jnp.concatenate([jnp.where(col_rank < 8, seat, -1), jnp.where(col_rank < 8, -1, seat)], axis=0)
    w = jnp.where(seat[:, 0:1] == jnp.bitwise_and(iota((64, 192), 1), 63), 1.0, 0.0)

    for c in replies:
        c.wait_recv()
    answer = jnp.concatenate([rp[:, c].reshape(nr * 8, 128) for c in range(3)], axis=1)
    spread = pick(w, pieces(answer))
    u = []
    for c in range(3):
        lo, hi = spread[0:32, 128 * c : 128 * c + 128], spread[32:64, 128 * c : 128 * c + 128]
        even = lo[0:16] + pltpu.roll(hi[0:16], 64, axis=1)
        odd = pltpu.roll(lo[16:32], 64, axis=1) + hi[16:32]
        u.append(uown[c] + jnp.where(low16, even, odd))

    cross_ax = jnp.zeros((8, 128), F32)
    cross_rad = jnp.zeros((8, 128), F32)
    tile_ax, lane_ax = jnp.right_shift(list_ax, 7), jnp.bitwise_and(list_ax, 127)
    tile_rad, lane_rad = jnp.right_shift(list_rad, 7), jnp.bitwise_and(list_rad, 127)
    for t in range(16):
        row = lambda x: jnp.broadcast_to(x[t : t + 1, :], (8, 128))
        old = jnp.concatenate([pmv[:, 128 * t : 128 * t + 128], jnp.zeros((2, 128), F32)], axis=0)
        gas_t = jnp.where(sub8 == 3, row(u[0]), jnp.where(sub8 == 4, row(u[1]), row(u[2])))
        vel = gas_t + (old - gas_t) * row(factor)
        pos = old + 0.5 * pltpu.roll(vel, 5, axis=0)
        new = jnp.where(sub8 < 3, pos, jnp.where(is_vel, vel, row(size)))
        motv[:, 128 * t : 128 * t + 128] = new[0:6]
        cross_ax = jnp.where(tile_ax == t, lane_gather(new, lane_ax), cross_ax)
        cross_rad = jnp.where(tile_rad == t, lane_gather(new, lane_rad), cross_rad)
    cross_ax = jnp.where(live_ax, cross_ax, 0.0)
    cross_rad = jnp.where(live_rad, cross_rad, 0.0)
    xs[0] = cross_ax
    xs[1] = pltpu.roll(cross_ax, 64, axis=1)
    xs[2] = cross_rad
    xs[3] = pltpu.roll(cross_rad, 64, axis=1)

    def crossing(i):
        dst = (xa.at[0], xa.at[1], xr.at[0], xr.at[1])[i]
        where = ({"ax": a + 1}, {"ax": a - 1}, {"rad": r + 1}, {"rad": r - 1})[i]
        return to(xs.at[i], dst, x_s.at[i], x_r.at[i], **where)

    @pl.when(core == 1)
    def _():
        pl.semaphore_wait(barrier, 2 * (has_prev.astype(I32) + has_next.astype(I32)))
        pl.semaphore_signal(ax_go, inc=1, device_id={"rad": sibling}, device_id_type=MESH)

    @pl.when(core == 0)
    def _():
        pl.semaphore_wait(ax_go, 1)

    sends_to = (has_next, has_prev, has_out, has_in)
    comes_from = (has_prev, has_next, has_in, has_out)
    for i in range(4):

        @pl.when(sends_to[i])
        def _(i=i):
            crossing(i).start()

    @pl.when(has_next)
    def _():
        halo_next().start()

    @pl.when(has_prev)
    def _():
        halo_prev().start()

    loads[8].wait()
    for c in shares[:1] + share_again:
        c.wait_recv()
    slab_rows = jnp.concatenate(
        [slab[:, :, 128 * q : 128 * q + 128].reshape(nr * 16, 128) for q in range(4)], axis=0
    )
    p3[...] = jnp.concatenate(split3(slab_rows), axis=1)
    three = jnp.dot(chosen[...], p3[...], preferred_element_type=F32)
    grouped = three[:, 0:128] + three[:, 128:256] + three[:, 256:384]
    high = grouped.astype(BF16)
    low = (grouped - high.astype(F32)).astype(BF16)
    high = jnp.concatenate([high[64 * t : 64 * t + 64] for t in range(8)], axis=1)
    low = jnp.concatenate([low[64 * t : 64 * t + 64] for t in range(8)], axis=1)
    coup[...] = lax.dot_general(
        jnp.concatenate([high, low, high], axis=1), tab3[...], NT_DIMS, preferred_element_type=F32
    )

    deposit_again = pass_on(deposits, sd, sd_s, sd_r)

    for c in deposits[:1] + deposit_again:
        c.wait_recv()
    own_at = jnp.broadcast_to(thrice(ident)[0:1, 0:96], (64, 96))
    far_at = jnp.broadcast_to(jnp.concatenate([asked] * 3, axis=1), (64, 384))
    hits_own = jnp.where(own_at == r * 64 + iota((64, 96), 0), 1.0, 0.0)
    hits_far = jnp.where(far_at == r * 64 + 1 + iota((64, 384), 0), 1.0, 0.0)
    far = jnp.concatenate([sd[:, c].reshape(nr * SLOTS, 128) for c in range(ROWS)], axis=1)
    sources = pick(hits_own, own3) + pick(hits_far, pieces(far))
    for q in range(4):
        rows = slice(16 * q, 16 * q + 16)
        lanes = slice(128 * q, 128 * q + 128)
        weight = sources[rows, 0:128]
        for c in range(3):
            g = gasv[c, :, lanes]
            gasov[c, :, lanes] = g + (sources[rows, 128 * c + 128 : 128 * c + 256] - g * weight)
        liqv[:, lanes] = sources[rows, 512:640]

    @pl.when(has_prev)
    def _():
        to(pres.at[8:16], halo.at[0], ha_s.at[0], ha_r.at[0], ax=a - 1).wait_recv()

    @pl.when(has_next)
    def _():
        to(pres.at[0:8], halo.at[1], ha_s.at[1], ha_r.at[1], ax=a + 1).wait_recv()

    mine = slab[r]
    above = jnp.concatenate([halo[0, 7:8, :], mine[0:15]], axis=0)
    below = jnp.concatenate([mine[1:16], halo[1, 0:1, :]], axis=0)
    image = 6.0 * mine - below - above
    for q in range(4):
        lanes = slice(128 * q, 128 * q + 128)
        pimv[:, lanes] = image[:, lanes] + coup[pl.ds(q, 16, stride=4), :]

    for i in range(4):

        @pl.when(comes_from[i])
        def _(i=i):
            crossing(i).wait_recv()

    for i in range(2):
        for f in range(7):
            arrav[0, 0, f, i : i + 1, :] = xa[i, f : f + 1, 0:64]
            arrrv[0, 0, f, i : i + 1, :] = xr[i, f : f + 1, 0:32]
    for c in requests + replies + shares + deposits + share_again + deposit_again:
        c.wait_send()

    @pl.when(has_next)
    def _():
        halo_next().wait_send()

    @pl.when(has_prev)
    def _():
        halo_prev().wait_send()

    for i in range(4):

        @pl.when(sends_to[i])
        def _(i=i):
            crossing(i).wait_send()


def out_kernel(*refs):
    sources, targets, sem = refs[:6], refs[6:12], refs[12]
    copies = [pltpu.make_async_copy(s, t, sem.at[i]) for i, (s, t) in enumerate(zip(sources, targets))]
    for c in copies:
        c.start()
    for c in copies:
        c.wait()


def on_device(na, nr, pm, ps, pb, po, gas, pres, cols, kinds, table, sa, sr, sc):
    outs = (
        jax.ShapeDtypeStruct((6, 2048), F32),
        jax.ShapeDtypeStruct((1, 1, 7, 2, 64), F32),
        jax.ShapeDtypeStruct((1, 1, 7, 2, 32), F32),
        jax.ShapeDtypeStruct((3, 16, 512), F32),
        jax.ShapeDtypeStruct((16, 512), F32),
        jax.ShapeDtypeStruct((16, 512), F32),
    )
    V = pltpu.VMEM
    dma = pltpu.SemaphoreType.DMA
    anyspec = pl.BlockSpec(memory_space=pltpu.HBM)
    scratch = [
        V((6, 2048), F32),
        V((16, 128), F32),
        V((1, 32), I32),
        V((16, 128), I32),
        V((3, 16, 512), F32),
        V((1, 4, 64), I32),
        V((1, 4, 64), I32),
        V((8, 128, 128), F32),
        V((1, 1, 2, 64), I32),
        V((1, 1, 2, 32), I32),
        V((1, 1, 4), I32),
        V((nr, 16, 512), F32),
        V((8, 128), I32),
        V((nr, 16, 128), I32),
        V((16, 128), I32),
        V((nr, 3, 8, 128), F32),
        V((nr, 3, 8, 128), F32),
        V((3, 16, 128), F32),
        V((32, 8, 128), F32),
        V((nr, ROWS, SLOTS, 128), F32),
        V((ROWS, SLOTS, 128), F32),
        V((2, 8, 512), F32),
        V((4, 8, 128), F32),
        V((2, 8, 128), F32),
        V((2, 8, 128), F32),
        V((4, 64, 128), I32),
        V((64, 128), F32),
        V((512, 384), BF16),
        V((512, 512), BF16),
        V((128, 3072), BF16),
        dma((12,)),
        dma((8,)),
        dma((8,)),
        dma((8,)),
        dma((8,)),
        dma((8,)),
        dma((8,)),
        dma((8,)),
        dma((8,)),
        dma((2,)),
        dma((2,)),
        dma((4,)),
        dma((4,)),
        pltpu.SemaphoreType.REGULAR,
        pltpu.SemaphoreType.REGULAR,
    ]
    parts = pl.pallas_call(
        functools.partial(step_kernel, na, nr),
        out_shape=[pltpu.VMEM(o.shape, o.dtype) for o in outs],
        in_specs=[anyspec] * 12,
        out_specs=[pl.BlockSpec(memory_space=pltpu.VMEM)] * 6,
        scratch_shapes=scratch,
        compiler_params=pltpu.CompilerParams(
            collective_id=0, has_side_effects=True, vmem_limit_bytes=VMEM_BYTES
        ),
        name="step",
    )(
        pm,
        ps.reshape(16, 128),
        pb.reshape(1, 32),
        po.reshape(16, 128),
        gas,
        pres,
        jnp.swapaxes(cols, 1, 2),
        jnp.swapaxes(kinds, 1, 2),
        table,
        sa,
        sr,
        sc,
    )
    motion, axial, radial, gas_out, load, image = pl.pallas_call(
        out_kernel,
        out_shape=outs,
        in_specs=[pl.BlockSpec(memory_space=pltpu.VMEM)] * 6,
        out_specs=[anyspec] * 6,
        scratch_shapes=[dma((6,))],
        compiler_params=pltpu.CompilerParams(vmem_limit_bytes=1024 * 1024),
        name="copy_out",
    )(*parts)
    return motion, jnp.swapaxes(axial, 2, 3), jnp.swapaxes(radial, 2, 3), gas_out, load, image


def solution(mesh):
    na, nr = mesh.shape["ax"], mesh.shape["rad"]
    return jax.shard_map(
        functools.partial(on_device, na, nr),
        mesh=mesh,
        in_specs=(
            P(None, ("ax", "rad")),
            P(("ax", "rad")),
            P(("ax", "rad")),
            P(("ax", "rad")),
            P(None, "ax", "rad"),
            P("ax", "rad"),
            P("ax", "rad", None),
            P("ax", "rad", None),
            P(),
            P("ax", "rad", None, None),
            P("ax", "rad", None, None),
            P("ax", "rad", None),
        ),
        out_specs=(
            P(None, ("ax", "rad")),
            P("ax", "rad", None, None, None),
            P("ax", "rad", None, None, None),
            P(None, "ax", "rad"),
            P("ax", "rad"),
            P("ax", "rad"),
        ),
        check_vma=False,
    )
```

```python
import functools

import jax
import jax.numpy as jnp
from jax import lax
from jax.experimental import pallas as pl
from jax.experimental.pallas import tpu as pltpu
from jax.sharding import PartitionSpec as P

MESH = pl.DeviceIdType.MESH
F32 = jnp.float32
BF16 = jnp.bfloat16
I32 = jnp.int32
HIGHEST = lax.Precision.HIGHEST
SLOTS = 16
ROWS = 5
VMEM_BYTES = 62 * 1024 * 1024
NT_DIMS = (((1,), (1,)), ((), ()))


def hdot(a, b):
    return jnp.dot(a, b, precision=HIGHEST, preferred_element_type=F32)


def split3(x):
    hi = x.astype(BF16)
    rest = x - hi.astype(F32)
    mid = rest.astype(BF16)
    lo = (rest - mid.astype(F32)).astype(BF16)
    return hi, mid, lo


def pieces(x):
    return jnp.concatenate(split3(x), axis=0)


def pick(onehot, x3):
    return jnp.dot(onehot.astype(BF16), x3, preferred_element_type=F32)


def iota(shape, dim):
    return lax.broadcasted_iota(I32, shape, dim)


def lane_gather(x, index):
    return jnp.take_along_axis(x, index, axis=1)


def step_kernel(
    na,
    nr,
    pm,
    ps,
    pb,
    po,
    gas,
    pres,
    cols,
    kinds,
    table,
    sa,
    sr,
    sc,
    motv,
    arrav,
    arrrv,
    gasov,
    liqv,
    pimv,
    pmv,
    psv,
    pbv,
    pov,
    gasv,
    colv,
    kindv,
    tabv,
    sav,
    srv,
    scv,
    slab,
    rows8,
    rq,
    rqs,
    rp,
    rps,
    uown,
    dp,
    raw,
    raw_out,
    vt,
    st,
    df,
    halo,
    xs,
    xa,
    xr,
    keys,
    coup,
    p3,
    chosen,
    tab3,
    lsem,
    rq_s,
    rq_r,
    rp_s,
    rp_r,
    pr_s,
    pr_r,
    sd_s,
    sd_r,
    ha_s,
    ha_r,
    x_s,
    x_r,
    slab_go,
    ax_go,
):
    a = lax.axis_index("ax")
    r = lax.axis_index("rad")
    has_prev, has_next = a > 0, a < na - 1
    has_in, has_out = r > 0, r < nr - 1

    def to(src, dst, ssem, rsem, **where):
        return pltpu.make_async_remote_copy(
            src_ref=src, dst_ref=dst, send_sem=ssem, recv_sem=rsem, device_id=where, device_id_type=MESH
        )

    core = lax.rem(r, 2)
    sibling = r + 1 - 2 * core
    barrier = pltpu.get_barrier_semaphore()
    for k in range(1, 4):
        even = lax.rem(r - core + 2 * k, nr)
        pl.semaphore_signal(barrier, inc=1, device_id={"rad": even}, device_id_type=MESH)

    @pl.when(core == 1)
    def _():
        pl.semaphore_signal(barrier, inc=1, device_id={"rad": sibling}, device_id_type=MESH)

    @pl.when(has_prev)
    def _():
        pl.semaphore_signal(barrier, inc=1, device_id={"ax": a - 1, "rad": r - core + 1}, device_id_type=MESH)

    @pl.when(has_next)
    def _():
        pl.semaphore_signal(barrier, inc=1, device_id={"ax": a + 1, "rad": r - core + 1}, device_id_type=MESH)

    loads = [
        pltpu.make_async_copy(src, dst, lsem.at[i])
        for i, (src, dst) in enumerate(
            (
                (pb, pbv),
                (po, pov),
                (gas, gasv),
                (ps, psv),
                (pm, pmv),
                (sa, sav),
                (sr, srv),
                (sc, scv),
                (pres, slab.at[r]),
                (cols, colv),
                (kinds, kindv),
                (table, tabv),
            )
        )
    ]
    for load in loads:
        load.start()

    lane8 = iota((8, 128), 1)
    sub8 = iota((8, 128), 0)
    lane16 = iota((16, 128), 1)
    low8 = lane8 < 64
    low16 = lane16 < 64

    rows8[...] = jnp.zeros((8, 128), I32)
    loads[0].wait()
    loads[1].wait()
    rows8[0:1, 0:32] = pbv[...]
    blocks = jnp.broadcast_to(rows8[0:1, :], (8, 128))
    order = jnp.bitwise_and(jnp.where(lane8 < 16, 2 * lane8, 2 * lane8 - 31), 127)
    blocks = lane_gather(blocks, order)
    owner = jnp.right_shift(blocks, 6)
    local = jnp.bitwise_and(blocks, 63)
    ident = owner * 64 + jnp.bitwise_and(local, 3) * 16 + jnp.right_shift(local, 2)
    valid = lane8 < 32

    def thrice(x):
        return jnp.where(lane8 < 32, x, jnp.where(lane8 < 64, pltpu.roll(x, 32, axis=1), pltpu.roll(x, 64, axis=1)))

    away = jnp.where(valid & (owner != r), 1, 0)
    rank = away
    for s in (1, 2, 4, 8, 16):
        rank = rank + jnp.where(lane8 >= s, pltpu.roll(rank, s, axis=1), 0)
    rank = rank - away
    row_rank = jnp.where(away > 0, rank, -1)
    code = jnp.where(valid, (rank * 2 + away) * 1024 + ident, 0)
    col = jnp.transpose(jnp.broadcast_to(code[0:1, :], (128, 128)))[0:32, :]
    col_id = jnp.bitwise_and(col, 1023)
    col_away = jnp.bitwise_and(jnp.right_shift(col, 10), 1)
    col_rank = jnp.right_shift(col, 11)
    lane32 = iota((32, 128), 1)
    picked = jnp.where((col_away > 0) & (col_rank + SLOTS * r == lane32), col_id + 1, 0)
    ids = picked[0:8] + picked[8:16] + picked[16:24] + picked[24:32]
    for s in (4, 2, 1):
        ids = ids + pltpu.roll(ids, s, axis=0)
    to_slot = jnp.where(
        jnp.broadcast_to(row_rank[0:1, :], (SLOTS, 128)) == iota((SLOTS, 128), 0), 1.0, 0.0
    ).astype(F32)[:, 0:32]
    offsets = pov[...]
    offs_f = offsets.astype(F32)
    slot_offs = jnp.dot(
        to_slot.astype(BF16),
        jnp.concatenate([offs_f, pltpu.roll(offs_f, 64, axis=1)], axis=0).astype(BF16),
        preferred_element_type=F32,
    ).astype(I32)
    rqs[0:8, :] = jnp.where(low8, slot_offs[0:8], pltpu.roll(slot_offs[8:16], 64, axis=1))
    rqs[8:9, :] = ids[0:1]

    rq[r] = jnp.zeros((16, 128), I32)
    rp[r] = jnp.zeros((3, 8, 128), F32)
    raw[r] = jnp.zeros((4, 8, 128), F32)

    @pl.when(jnp.logical_not(has_prev))
    def _():
        xa[0] = jnp.zeros((8, 128), F32)
        halo[0] = jnp.zeros((8, 512), F32)

    @pl.when(jnp.logical_not(has_next))
    def _():
        xa[1] = jnp.zeros((8, 128), F32)
        halo[1] = jnp.zeros((8, 512), F32)

    @pl.when(jnp.logical_not(has_in))
    def _():
        xr[0] = jnp.zeros((8, 128), F32)

    @pl.when(jnp.logical_not(has_out))
    def _():
        xr[1] = jnp.zeros((8, 128), F32)

    @pl.when(core == 0)
    def _():
        pl.semaphore_wait(barrier, nr - 1)
        pl.semaphore_signal(slab_go, inc=1, device_id={"rad": sibling}, device_id_type=MESH)

    @pl.when(core == 1)
    def _():
        pl.semaphore_wait(slab_go, 1)

    def spread_out(src, dst, ssem, rsem):
        copies = []
        for j in range(4):
            target = lax.rem(r + 2 * j, nr) if j else sibling
            c = to(src, dst.at[r], ssem.at[j], rsem.at[j], rad=target)
            c.start()
            copies.append(c)
        return copies

    def pass_on(copies, dst, ssem, rsem):
        again = []
        for j in range(1, 4):
            copies[j].wait_recv()
            origin = dst.at[lax.rem(r + nr - 2 * j, nr)]
            c = to(origin, origin, ssem.at[3 + j], rsem.at[3 + j], rad=sibling)
            c.start()
            again.append(c)
        return again

    requests = []
    for k in range(1, nr):
        c = to(rqs.at[0:9], rq.at[r, 0:9], rq_s.at[k], rq_r.at[k], rad=lax.rem(r + k, nr))
        c.start()
        requests.append(c)


    def halo_next():
        return to(pres.at[8:16], halo.at[0], ha_s.at[0], ha_r.at[0], ax=a + 1)

    def halo_prev():
        return to(pres.at[0:8], halo.at[1], ha_s.at[1], ha_r.at[1], ax=a - 1)

    loads[3].wait()
    size = psv[...]
    loads[4].wait()
    for t in range(16):
        vt[:, t, :] = pmv[3:6, 128 * t : 128 * t + 128]
    flat = jnp.concatenate([vt[0], vt[1], vt[2], size], axis=1)
    turned = [pltpu.roll(x, 64, axis=1) for x in (vt[0], vt[1], vt[2], size)]
    flat = pieces(jnp.concatenate([flat, jnp.concatenate(turned, axis=1)], axis=0))
    slot_of = jnp.broadcast_to(thrice(row_rank)[0:1, 0:96], (SLOTS, 96))
    flat = pick(jnp.where(slot_of == iota((SLOTS, 96), 0), 1.0, 0.0), flat)
    for c in range(4):
        part = flat[:, 128 * c : 128 * c + 128]
        raw_out[c] = jnp.where(low8, part[0:8], pltpu.roll(part[8:16], 64, axis=1))
    raws = spread_out(raw_out, raw, sd_s, sd_r)
    shares = spread_out(pres, slab, pr_s, pr_r)

    loads[2].wait()
    gas_rows = jnp.concatenate(
        [
            jnp.concatenate([gasv[c, :, 128 * q : 128 * q + 128] for q in range(4)], axis=0)
            for c in range(3)
        ],
        axis=1,
    )
    gas3 = pieces(gas_rows)
    at_own = jnp.where(col_id[:, 0:1] == r * 64 + jnp.bitwise_and(iota((32, 192), 1), 63), 1.0, 0.0)
    found = pick(at_own, gas3)
    for c in range(3):
        part = found[:, 128 * c : 128 * c + 128]
        uown[c] = jnp.where(low16, lane_gather(part[0:16], offsets), lane_gather(part[16:32], offsets))

    for c in requests:
        c.wait_recv()
    asked = rq[0, 8:9, :]
    for s in range(1, nr):
        asked = asked + rq[s, 8:9, :]
    asked_col = jnp.transpose(jnp.broadcast_to(asked[0:1, :], (128, 128)))
    at_asked = jnp.where(asked_col[:, 0:1] == r * 64 + 1 + jnp.bitwise_and(iota((128, 192), 1), 63), 1.0, 0.0)
    found = pick(at_asked, gas3)
    for s in range(nr):
        index = rq[s, 0:8, :]
        for c in range(3):
            part = found[SLOTS * s : SLOTS * s + 16, 128 * c : 128 * c + 128]
            rps[s, c] = jnp.where(low8, lane_gather(part[0:8], index), lane_gather(part[8:16], index))
    replies = []
    for k in range(1, nr):
        dst = lax.rem(r + k, nr)
        c = to(rps.at[dst], rp.at[r], rp_s.at[k], rp_r.at[k], rad=dst)
        c.start()
        replies.append(c)
    factor = jnp.exp(-0.5 / (size * size))
    mass = size * size * size
    share = mass * (1.0 - factor)
    is_vel = (sub8 >= 3) & (sub8 < 6)
    sub128 = iota((128, 128), 0)
    for t in range(16):
        row = lambda x: jnp.broadcast_to(x[t : t + 1, :], (8, 128))
        old = jnp.concatenate([pmv[:, 128 * t : 128 * t + 128], jnp.zeros((2, 128), F32)], axis=0)
        d = row(share) * jnp.where(is_vel, old, 1.0)
        d = jnp.where(sub8 == 6, row(mass), d)
        both = jnp.concatenate([jnp.where(low8, d, 0.0), jnp.where(low8, 0.0, d)], axis=0)
        cells = jnp.where(jnp.broadcast_to(offsets[t : t + 1, :], (128, 128)) == sub128, 1.0, 0.0).astype(BF16)
        sums = lax.dot_general(pieces(both), cells, NT_DIMS, preferred_element_type=F32)
        sums = sums[0:16] + sums[16:32] + sums[32:48]
        dp[t] = sums[0:8]
        dp[16 + t] = sums[8:16]
    own3 = pieces(jnp.concatenate([dp[:, 2 + c, :] for c in range(ROWS)], axis=1))

    raw_again = pass_on(raws, raw, sd_s, sd_r)
    share_again = pass_on(shares, slab, pr_s, pr_r)

    loads[9].wait()
    loads[10].wait()
    cv = colv[0]
    key = kindv[0] * 512 + jnp.bitwise_and(cv, 3) * 128 + jnp.right_shift(cv, 6) * 16
    key = key + jnp.bitwise_and(jnp.right_shift(cv, 2), 15)
    rows8[4:8, 0:64] = key
    for k in range(4):
        keys[k] = jnp.transpose(jnp.broadcast_to(rows8[4 + k : 5 + k, :], (128, 128)))[0:64, :]
    lane64 = iota((64, 128), 1)

    def choose(t, carry):
        for q in range(4):
            want = t * 512 + q * 128 + lane64
            g = jnp.where(keys[0] == want, 1.0, 0.0)
            for k in range(1, 4):
                g = g + jnp.where(keys[k] == want, 1.0, 0.0)
            chosen[pl.ds(pl.multiple_of(64 * t, 64), 64), 128 * q : 128 * q + 128] = g.astype(BF16)
        return carry

    lax.fori_loop(0, 8, choose, 0)
    loads[11].wait()
    for t in range(8):
        tab = tabv[t]
        tab_high = tab.astype(BF16)
        tab3[:, 128 * t : 128 * t + 128] = tab_high
        tab3[:, 1024 + 128 * t : 1152 + 128 * t] = tab_high
        tab3[:, 2048 + 128 * t : 2176 + 128 * t] = (tab - tab_high.astype(F32)).astype(BF16)

    for i in (5, 6, 7):
        loads[i].wait()
    rows8[0:2, 0:64] = sav[0, 0]
    rows8[2:4, 0:32] = srv[0, 0]
    lists = [jnp.broadcast_to(rows8[i : i + 1, :], (8, 128)) for i in range(4)]
    counts = [jnp.broadcast_to(scv[0, :, i : i + 1], (8, 128)) for i in range(4)]
    list_ax = jnp.where(low8, lists[0], pltpu.roll(lists[1], 64, axis=1))
    list_rad = jnp.where(low8, lists[2], pltpu.roll(lists[3], 64, axis=1))
    live_ax = lane8 < jnp.where(low8, counts[0], counts[1] + 64)
    live_rad = lane8 < jnp.where(low8, counts[2], counts[3] + 64)

    seat = jnp.where(col_away > 0, jnp.right_shift(col_id, 6) * 8 + jnp.bitwise_and(col_rank, 7), -1)
    seat = jnp.concatenate([jnp.where(col_rank < 8, seat, -1), jnp.where(col_rank < 8, -1, seat)], axis=0)
    w = jnp.where(seat[:, 0:1] == jnp.bitwise_and(iota((64, 192), 1), 63), 1.0, 0.0)

    for c in replies:
        c.wait_recv()
    answer = jnp.concatenate([rp[:, c].reshape(nr * 8, 128) for c in range(3)], axis=1)
    spread = pick(w, pieces(answer))
    u = []
    for c in range(3):
        lo, hi = spread[0:32, 128 * c : 128 * c + 128], spread[32:64, 128 * c : 128 * c + 128]
        even = lo[0:16] + pltpu.roll(hi[0:16], 64, axis=1)
        odd = pltpu.roll(lo[16:32], 64, axis=1) + hi[16:32]
        u.append(uown[c] + jnp.where(low16, even, odd))

    cross_ax = jnp.zeros((8, 128), F32)
    cross_rad = jnp.zeros((8, 128), F32)
    tile_ax, lane_ax = jnp.right_shift(list_ax, 7), jnp.bitwise_and(list_ax, 127)
    tile_rad, lane_rad = jnp.right_shift(list_rad, 7), jnp.bitwise_and(list_rad, 127)
    for t in range(16):
        row = lambda x: jnp.broadcast_to(x[t : t + 1, :], (8, 128))
        old = jnp.concatenate([pmv[:, 128 * t : 128 * t + 128], jnp.zeros((2, 128), F32)], axis=0)
        gas_t = jnp.where(sub8 == 3, row(u[0]), jnp.where(sub8 == 4, row(u[1]), row(u[2])))
        vel = gas_t + (old - gas_t) * row(factor)
        pos = old + 0.5 * pltpu.roll(vel, 5, axis=0)
        new = jnp.where(sub8 < 3, pos, jnp.where(is_vel, vel, row(size)))
        motv[:, 128 * t : 128 * t + 128] = new[0:6]
        cross_ax = jnp.where(tile_ax == t, lane_gather(new, lane_ax), cross_ax)
        cross_rad = jnp.where(tile_rad == t, lane_gather(new, lane_rad), cross_rad)
    cross_ax = jnp.where(live_ax, cross_ax, 0.0)
    cross_rad = jnp.where(live_rad, cross_rad, 0.0)
    xs[0] = cross_ax
    xs[1] = pltpu.roll(cross_ax, 64, axis=1)
    xs[2] = cross_rad
    xs[3] = pltpu.roll(cross_rad, 64, axis=1)

    def crossing(i):
        dst = (xa.at[0], xa.at[1], xr.at[0], xr.at[1])[i]
        where = ({"ax": a + 1}, {"ax": a - 1}, {"rad": r + 1}, {"rad": r - 1})[i]
        return to(xs.at[i], dst, x_s.at[i], x_r.at[i], **where)

    @pl.when(core == 1)
    def _():
        pl.semaphore_wait(barrier, 2 * (has_prev.astype(I32) + has_next.astype(I32)))
        pl.semaphore_signal(ax_go, inc=1, device_id={"rad": sibling}, device_id_type=MESH)

    @pl.when(core == 0)
    def _():
        pl.semaphore_wait(ax_go, 1)

    sends_to = (has_next, has_prev, has_out, has_in)
    comes_from = (has_prev, has_next, has_in, has_out)
    for i in range(4):

        @pl.when(sends_to[i])
        def _(i=i):
            crossing(i).start()

    @pl.when(has_next)
    def _():
        halo_next().start()

    @pl.when(has_prev)
    def _():
        halo_prev().start()

    for c in raws[:1] + raw_again:
        c.wait_recv()
    blank = jnp.zeros((8, 128), F32)
    df[pl.ds(pl.multiple_of(SLOTS * r, SLOTS), SLOTS)] = jnp.zeros((SLOTS, 8, 128), F32)
    for k in range(1, nr):
        s = lax.rem(r + k, nr)
        d = raw[s, 3]
        m = d * d * d
        k_ = m * (1.0 - jnp.exp(-0.5 / (d * d)))
        values = [k_, k_ * raw[s, 0], k_ * raw[s, 1], k_ * raw[s, 2], m]
        for c in range(8):
            value = values[c] if c < ROWS else blank
            hi = value.astype(BF16).astype(F32) if c < ROWS else blank
            lo = value - hi if c < ROWS else blank
            for i, piece in enumerate((hi, lo)):
                st[k, 16 * i + c] = jnp.where(low8, piece, 0.0) if c < ROWS else blank
                st[k, 16 * i + 8 + c] = jnp.where(low8, 0.0, piece) if c < ROWS else blank
        for i in range(8):
            cells = jnp.where(jnp.broadcast_to(rq[s, i : i + 1, :], (128, 128)) == sub128, 1.0, 0.0).astype(BF16)
            sums = lax.dot_general(st[k, :, i, :].astype(BF16), cells, NT_DIMS, preferred_element_type=F32)
            sums = sums[0:16] + sums[16:32]
            df[SLOTS * s + i] = sums[0:8]
            df[SLOTS * s + 8 + i] = sums[8:16]

    loads[8].wait()
    for c in shares[:1] + share_again:
        c.wait_recv()
    slab_rows = jnp.concatenate(
        [slab[:, :, 128 * q : 128 * q + 128].reshape(nr * 16, 128) for q in range(4)], axis=0
    )
    p3[...] = jnp.concatenate(split3(slab_rows), axis=1)
    three = jnp.dot(chosen[...], p3[...], preferred_element_type=F32)
    grouped = three[:, 0:128] + three[:, 128:256] + three[:, 256:384]
    high = grouped.astype(BF16)
    low = (grouped - high.astype(F32)).astype(BF16)
    high = jnp.concatenate([high[64 * t : 64 * t + 64] for t in range(8)], axis=1)
    low = jnp.concatenate([low[64 * t : 64 * t + 64] for t in range(8)], axis=1)
    coup[...] = lax.dot_general(
        jnp.concatenate([high, low, high], axis=1), tab3[...], NT_DIMS, preferred_element_type=F32
    )

    own_at = jnp.broadcast_to(thrice(ident)[0:1, 0:96], (64, 96))
    far_at = jnp.broadcast_to(jnp.concatenate([asked] * 3, axis=1), (64, 384))
    hits_own = jnp.where(own_at == r * 64 + iota((64, 96), 0), 1.0, 0.0)
    hits_far = jnp.where(far_at == r * 64 + 1 + iota((64, 384), 0), 1.0, 0.0)
    far = jnp.concatenate([df[:, c, :] for c in range(ROWS)], axis=1)
    sources = pick(hits_own, own3) + pick(hits_far, pieces(far))
    for q in range(4):
        rows = slice(16 * q, 16 * q + 16)
        lanes = slice(128 * q, 128 * q + 128)
        weight = sources[rows, 0:128]
        for c in range(3):
            g = gasv[c, :, lanes]
            gasov[c, :, lanes] = g + (sources[rows, 128 * c + 128 : 128 * c + 256] - g * weight)
        liqv[:, lanes] = sources[rows, 512:640]

    @pl.when(has_prev)
    def _():
        to(pres.at[8:16], halo.at[0], ha_s.at[0], ha_r.at[0], ax=a - 1).wait_recv()

    @pl.when(has_next)
    def _():
        to(pres.at[0:8], halo.at[1], ha_s.at[1], ha_r.at[1], ax=a + 1).wait_recv()

    mine = slab[r]
    above = jnp.concatenate([halo[0, 7:8, :], mine[0:15]], axis=0)
    below = jnp.concatenate([mine[1:16], halo[1, 0:1, :]], axis=0)
    image = 6.0 * mine - below - above
    for q in range(4):
        lanes = slice(128 * q, 128 * q + 128)
        pimv[:, lanes] = image[:, lanes] + coup[pl.ds(q, 16, stride=4), :]

    for i in range(4):

        @pl.when(comes_from[i])
        def _(i=i):
            crossing(i).wait_recv()

    for i in range(2):
        for f in range(7):
            arrav[0, 0, f, i : i + 1, :] = xa[i, f : f + 1, 0:64]
            arrrv[0, 0, f, i : i + 1, :] = xr[i, f : f + 1, 0:32]
    for c in requests + replies + shares + raws + share_again + raw_again:
        c.wait_send()

    @pl.when(has_next)
    def _():
        halo_next().wait_send()

    @pl.when(has_prev)
    def _():
        halo_prev().wait_send()

    for i in range(4):

        @pl.when(sends_to[i])
        def _(i=i):
            crossing(i).wait_send()


def out_kernel(*refs):
    sources, targets, sem = refs[:6], refs[6:12], refs[12]
    copies = [pltpu.make_async_copy(s, t, sem.at[i]) for i, (s, t) in enumerate(zip(sources, targets))]
    for c in copies:
        c.start()
    for c in copies:
        c.wait()


def on_device(na, nr, pm, ps, pb, po, gas, pres, cols, kinds, table, sa, sr, sc):
    outs = (
        jax.ShapeDtypeStruct((6, 2048), F32),
        jax.ShapeDtypeStruct((1, 1, 7, 2, 64), F32),
        jax.ShapeDtypeStruct((1, 1, 7, 2, 32), F32),
        jax.ShapeDtypeStruct((3, 16, 512), F32),
        jax.ShapeDtypeStruct((16, 512), F32),
        jax.ShapeDtypeStruct((16, 512), F32),
    )
    V = pltpu.VMEM
    dma = pltpu.SemaphoreType.DMA
    anyspec = pl.BlockSpec(memory_space=pltpu.HBM)
    scratch = [
        V((6, 2048), F32),
        V((16, 128), F32),
        V((1, 32), I32),
        V((16, 128), I32),
        V((3, 16, 512), F32),
        V((1, 4, 64), I32),
        V((1, 4, 64), I32),
        V((8, 128, 128), F32),
        V((1, 1, 2, 64), I32),
        V((1, 1, 2, 32), I32),
        V((1, 1, 4), I32),
        V((nr, 16, 512), F32),
        V((8, 128), I32),
        V((nr, 16, 128), I32),
        V((16, 128), I32),
        V((nr, 3, 8, 128), F32),
        V((nr, 3, 8, 128), F32),
        V((3, 16, 128), F32),
        V((32, 8, 128), F32),
        V((nr, 4, 8, 128), F32),
        V((4, 8, 128), F32),
        V((3, 16, 128), F32),
        V((nr, 32, 8, 128), F32),
        V((nr * SLOTS, 8, 128), F32),
        V((2, 8, 512), F32),
        V((4, 8, 128), F32),
        V((2, 8, 128), F32),
        V((2, 8, 128), F32),
        V((4, 64, 128), I32),
        V((64, 128), F32),
        V((512, 384), BF16),
        V((512, 512), BF16),
        V((128, 3072), BF16),
        dma((12,)),
        dma((8,)),
        dma((8,)),
        dma((8,)),
        dma((8,)),
        dma((8,)),
        dma((8,)),
        dma((8,)),
        dma((8,)),
        dma((2,)),
        dma((2,)),
        dma((4,)),
        dma((4,)),
        pltpu.SemaphoreType.REGULAR,
        pltpu.SemaphoreType.REGULAR,
    ]
    parts = pl.pallas_call(
        functools.partial(step_kernel, na, nr),
        out_shape=[pltpu.VMEM(o.shape, o.dtype) for o in outs],
        in_specs=[anyspec] * 12,
        out_specs=[pl.BlockSpec(memory_space=pltpu.VMEM)] * 6,
        scratch_shapes=scratch,
        compiler_params=pltpu.CompilerParams(
            collective_id=0, has_side_effects=True, vmem_limit_bytes=VMEM_BYTES
        ),
        name="step",
    )(
        pm,
        ps.reshape(16, 128),
        pb.reshape(1, 32),
        po.reshape(16, 128),
        gas,
        pres,
        jnp.swapaxes(cols, 1, 2),
        jnp.swapaxes(kinds, 1, 2),
        table,
        sa,
        sr,
        sc,
    )
    motion, axial, radial, gas_out, load, image = pl.pallas_call(
        out_kernel,
        out_shape=outs,
        in_specs=[pl.BlockSpec(memory_space=pltpu.VMEM)] * 6,
        out_specs=[anyspec] * 6,
        scratch_shapes=[dma((6,))],
        compiler_params=pltpu.CompilerParams(vmem_limit_bytes=1024 * 1024),
        name="copy_out",
    )(*parts)
    return motion, jnp.swapaxes(axial, 2, 3), jnp.swapaxes(radial, 2, 3), gas_out, load, image


def solution(mesh):
    na, nr = mesh.shape["ax"], mesh.shape["rad"]
    return jax.shard_map(
        functools.partial(on_device, na, nr),
        mesh=mesh,
        in_specs=(
            P(None, ("ax", "rad")),
            P(("ax", "rad")),
            P(("ax", "rad")),
            P(("ax", "rad")),
            P(None, "ax", "rad"),
            P("ax", "rad"),
            P("ax", "rad", None),
            P("ax", "rad", None),
            P(),
            P("ax", "rad", None, None),
            P("ax", "rad", None, None),
            P("ax", "rad", None),
        ),
        out_specs=(
            P(None, ("ax", "rad")),
            P("ax", "rad", None, None, None),
            P("ax", "rad", None, None, None),
            P(None, "ax", "rad"),
            P("ax", "rad"),
            P("ax", "rad"),
        ),
        check_vma=False,
    )
```
